512 devices in a mesh: group: 8 (over x, core), vocab: 64 (over y, z).
Axes of the slice: x: 4, y: 8, z: 8, core: 2. Of those that a mesh axis runs over, the one named last changes fastest.
Arguments:
- shard_ids: int32 [65536, 1], P(('group', 'vocab')), may hold values from 0 to 63; in each aligned block of 128 rows (0 to 127, 128 to 255, ...) at most 4 rows name the same one
- row_ids: int32 [65536], P(('group', 'vocab')), may hold values from 0 to 1001
- table: bfloat16 [64128, 4096], P('vocab', 'group'), may hold values from -6 to 6
- cotangent: bfloat16 [65536, 4096], P(('group', 'vocab')), may hold values from -6 to 6
Outputs:
- embeds: bfloat16 [65536, 4096], P(('group', 'vocab'))
- table_grad: bfloat16 [64128, 4096], P('vocab', 'group')
The draws below stay inside these ranges and needn't reach their ends.
Inputs may be any that keep to these rules, and one draw needn't show every extreme that they name: `shard_ids`: in each aligned block of 128 rows (the rows of one device), no shard is named by more than 4 rows, and in some blocks one shard is named by exactly 4.
All inputs are finite; a program needn't handle non-finite values.
Results may differ from the reference program's by a relative error of at most 0.001.
Values may be sent and summed in bfloat16 or wider, within the bound.
No kernel may reach another device: no remote copies, remote signals or barrier semaphores. Data moves between devices by JAX's collectives and lax.ppermute only.
A program may use at most 64 MiB of HBM per device.

```python
import math
import jax
import jax.numpy as jnp
import numpy as np

D = 4096
V = 64128
TOK_DEV = 128
TOKENS = 65536
SHARD_ROWS = 1002
CAP = 4
N_VOCAB = 64


def plant(result, key, smallest, largest):
    dims = result.shape
    spot = [jax.random.randint(jax.random.fold_in(key, axis), (), 0, dims[axis]) for axis in range(len(dims))]
    result = result.at[tuple(spot)].set(smallest)
    longest = dims.index(max(dims))
    spot[longest] = (spot[longest] + 1) % dims[longest]
    return result.at[tuple(spot)].set(largest)


def block_scale(own_key, extent, shards, low, top_value):
    def one(axis_at, shards_of):
        draws = jax.random.uniform(jax.random.fold_in(jax.random.fold_in(own_key, 6), axis_at), (shards_of,), jnp.float32, low / len(shards), top_value / len(shards))
        return jnp.repeat(jnp.exp(draws), extent[axis_at] // shards_of).reshape((-1,) + (1,) * (len(extent) - axis_at - 1))

    level = one(*shards[0])
    for cut in shards[1:]:
        level = level * one(*cut)
    return level


def cumulative_ranks(amount, skew):
    loads = [(1 << 20) // math.isqrt(standing ** skew) + 1 for standing in range(1, amount + 1)]
    deviation = 1 + sum(loads) // (1 << 30)
    return np.cumsum(np.array([max(1, weight // deviation) for weight in loads]))


def ranked(stream_key, shape, number_of, slope):
    grid = cumulative_ranks(number_of, slope)
    pick = jax.random.randint(jax.random.fold_in(stream_key, 1), shape, 0, int(grid[number_of - 1]))
    grade = jnp.searchsorted(jnp.asarray(grid, jnp.int32), pick, side="right")
    return jax.random.permutation(jax.random.fold_in(stream_key, 2), number_of)[grade].astype(jnp.int32)


def shared_out(own_key, own, number, rows, amount, top, reach, skew):
    sequence = jax.random.permutation(own_key, amount)
    crowded, usual = shares(amount, rows * top, reach, skew, True), shares(amount, rows * top, reach, skew, False)
    places = jnp.arange(amount)

    def named(tallies, rotation):
        used = int((tallies > 0).sum())
        fixed = max(1, used // 4)
        moved = fixed + (places - fixed + rotation * (used - fixed)) % max(1, amount - fixed)
        return jnp.zeros((amount,), jnp.int32).at[sequence[jnp.where(places < fixed, places, moved)]].set(jnp.asarray(tallies, jnp.int32))

    tallies = jnp.where(number % 4 == 0, named(crowded, number // 4), named(usual, number - number // 4 - 1))
    mixed = jax.random.permutation(jax.random.fold_in(own, 3), amount)
    giver, sink = mixed[0:amount // 2 * 2:2], mixed[1:amount // 2 * 2:2]
    slack = jnp.minimum(tallies[giver] - 1, reach - tallies[sink]) // 2
    slack = jnp.where((giver == sequence[0]) | (sink == sequence[0]) | (tallies[sink] == 0), 0, jnp.maximum(slack, 0))
    moved = jax.random.randint(jax.random.fold_in(own, 4), (amount // 2,), 0, 1 << 20) % (slack + 1)
    tallies = tallies.at[giver].add(-moved).at[sink].add(moved)
    items = jnp.searchsorted(jnp.cumsum(tallies), jnp.arange(rows * top), side="right").astype(jnp.int32)
    listing = items.reshape(top, rows).T
    listing = listing[jax.random.permutation(jax.random.fold_in(own, 1), rows)]
    rotation = jax.random.randint(jax.random.fold_in(own, 2), (rows, 1), 0, top)
    return jnp.take_along_axis(listing, (jnp.arange(top)[None, :] + rotation) % top, axis=1)


def shares(count, total, bound, lean, full):
    weights = [(1 << 20) // math.isqrt(rank ** lean) + 1 for rank in range(1, count + 1)]
    largest = bound if full else min(bound, max(-(-total // count), total * weights[0] // sum(weights)))
    least = 1 if total - largest >= count - 1 else 0
    counts, spare = [largest] + [least] * (count - 1), total - largest - least * (count - 1)
    while spare > 0:
        free = [i for i in range(1, count) if counts[i] < largest] or [i for i in range(1, count) if counts[i] < bound]
        mass, budget = sum([weights[i] for i in free]), spare
        for i in free:
            more = min(bound - counts[i], max(1, budget * weights[i] // mass), spare)
            counts[i] = counts[i] + more
            spare = spare - more
    return np.array(counts)


def centred(stream_key, shape, spread, most, split=(), dtype=jnp.bfloat16):
    loudness = block_scale(stream_key, shape, split, -0.22, 0.18) if split else 1.0
    entries = jax.random.normal(stream_key, shape, jnp.float32) * spread * loudness
    return jnp.minimum(jnp.maximum(entries, -most), most).astype(dtype)


def setup_inputs(seed: int = 0) -> dict:
    splits = jax.random.split(jax.random.key(seed), 5)
    shard_ids_keys = jax.random.split(jax.random.fold_in(splits[0], 1), TOKENS // TOK_DEV)
    shard_ids_turns = jax.random.permutation(jax.random.fold_in(splits[0], 3), TOKENS // TOK_DEV)
    shard_ids = jax.vmap(lambda own, number: shared_out(jax.random.fold_in(splits[0], 2), own, number, TOK_DEV, N_VOCAB, 1, CAP, 2))(shard_ids_keys, shard_ids_turns).reshape((TOKENS, 1))
    row_ids = plant(ranked(splits[1], (TOKENS,), SHARD_ROWS, 2), jax.random.fold_in(splits[1], 3), 0, SHARD_ROWS - 1).astype(jnp.int32)
    table = centred(splits[2], (V, D), 1.0, 6.0, ((0, 64), (1, 8)))
    cotangent = centred(splits[3], (TOKENS, D), 1.0, 6.0, ((0, 512),))
    return {"shard_ids": shard_ids, "row_ids": row_ids, "table": table, "cotangent": cotangent}


def reference(shard_ids, row_ids, table, cotangent):
    token_ids = (shard_ids[:, 0] * (V // N_VOCAB) + row_ids).astype(jnp.int32)
    embeds = jnp.take(table, token_ids, axis=0)
    summed = jax.ops.segment_sum(cotangent.astype(jnp.float32), token_ids, num_segments=V)
    return embeds, summed.astype(jnp.bfloat16)
```

```python
import functools

import jax
import jax.numpy as jnp
from jax import lax
from jax.experimental import pallas as pl
from jax.experimental.pallas import tpu as pltpu
from jax.sharding import PartitionSpec as P

LANES = 128


def to_column(row):
    n = row.shape[1]
    here = lax.broadcasted_iota(jnp.int32, (n, n), 0)
    there = lax.broadcasted_iota(jnp.int32, (n, n), 1)
    return jnp.sum(jnp.where(here == there, row, 0), axis=1, keepdims=True)


def pack_kernel(cap, pieces, owners, shard_ref, row_ref, cot_ref, out_ref, ids_ref, slot_ref, hot):
    tokens = shard_ref.shape[1]
    rows = hot.shape[0]

    @pl.when(pl.program_id(0) == 0)
    def _():
        shard = shard_ref[...]
        column = to_column(shard)
        i = lax.broadcasted_iota(jnp.int32, (tokens, tokens), 0)
        j = lax.broadcasted_iota(jnp.int32, (tokens, tokens), 1)
        earlier = jnp.where((column == shard) & (i < j), 1, 0)
        slot = shard * cap + jnp.sum(earlier, axis=0, keepdims=True)
        slot_ref[...] = slot
        target = lax.broadcasted_iota(jnp.int32, (tokens, owners * cap), 1)
        named = jnp.where(to_column(slot) == target, to_column(row_ref[...]) + 1, 0)
        ids_ref[...] = jnp.sum(named, axis=0, keepdims=True) - 1
        line = lax.broadcasted_iota(jnp.int32, (rows, tokens), 0)
        for c in range(pieces):
            hot[:, c * tokens : (c + 1) * tokens] = jnp.where(
                line == slot * pieces + c, 1.0, 0.0
            ).astype(jnp.bfloat16)

    groups = cot_ref.shape[1] // (pieces * LANES)
    right = []
    for g in range(groups):
        right.append(
            jnp.concatenate(
                [cot_ref[:, (g * pieces + c) * LANES : (g * pieces + c + 1) * LANES] for c in range(pieces)],
                axis=0,
            )
        )
    placed = jnp.dot(hot[...], jnp.concatenate(right, axis=1), preferred_element_type=jnp.float32)
    placed = placed.astype(jnp.bfloat16)
    for g in range(groups):
        block = placed[:, g * LANES : (g + 1) * LANES]
        out_ref[g * owners : (g + 1) * owners] = block.reshape(owners, rows // owners, LANES)


def pack(shard, row, cotangent, groups, owners, cap):
    tokens, width = cotangent.shape
    pieces = width // groups // LANES
    rows = owners * cap * pieces
    step = 2
    return pl.pallas_call(
        functools.partial(pack_kernel, cap, pieces, owners),
        grid=(groups // step,),
        in_specs=[
            pl.BlockSpec((1, tokens), lambda g: (0, 0)),
            pl.BlockSpec((1, tokens), lambda g: (0, 0)),
            pl.BlockSpec((tokens, step * pieces * LANES), lambda g: (0, g)),
        ],
        out_specs=[
            pl.BlockSpec((step * owners, cap * pieces, LANES), lambda g: (g, 0, 0)),
            pl.BlockSpec((1, owners * cap), lambda g: (0, 0)),
            pl.BlockSpec((1, tokens), lambda g: (0, 0)),
        ],
        out_shape=[
            jax.ShapeDtypeStruct((groups * owners, cap * pieces, LANES), jnp.bfloat16),
            jax.ShapeDtypeStruct((1, owners * cap), jnp.int32),
            jax.ShapeDtypeStruct((1, tokens), jnp.int32),
        ],
        scratch_shapes=[pltpu.VMEM((rows, pieces * tokens), jnp.bfloat16)],
        name="pack",
    )(shard, row, cotangent)


def unpack_kernel(pieces, slot_ref, got_ref, out_ref, hot):
    tokens = slot_ref.shape[1]
    rows = hot.shape[1]

    @pl.when(pl.program_id(0) == 0)
    def _():
        slot = to_column(slot_ref[...])
        line = lax.broadcasted_iota(jnp.int32, (tokens, rows), 1)
        for c in range(pieces):
            hot[c * tokens : (c + 1) * tokens, :] = jnp.where(
                line == slot * pieces + c, 1.0, 0.0
            ).astype(jnp.bfloat16)

    groups = out_ref.shape[1] // (pieces * LANES)
    owners = got_ref.shape[0] // groups
    right = [got_ref[g * owners : (g + 1) * owners].reshape(rows, LANES) for g in range(groups)]
    picked = jnp.dot(hot[...], jnp.concatenate(right, axis=1), preferred_element_type=jnp.float32)
    picked = picked.astype(jnp.bfloat16)
    for g in range(groups):
        for c in range(pieces):
            out_ref[:, (g * pieces + c) * LANES : (g * pieces + c + 1) * LANES] = picked[
                c * tokens : (c + 1) * tokens, g * LANES : (g + 1) * LANES
            ]


def unpack(slot, got, groups, width):
    tokens = slot.shape[1]
    pieces = width // groups // LANES
    owners = got.shape[0] // groups
    rows = owners * got.shape[1]
    step = 2
    return pl.pallas_call(
        functools.partial(unpack_kernel, pieces),
        grid=(groups // step,),
        in_specs=[
            pl.BlockSpec((1, tokens), lambda g: (0, 0)),
            pl.BlockSpec((step * owners, got.shape[1], LANES), lambda g: (g, 0, 0)),
        ],
        out_specs=pl.BlockSpec((tokens, step * pieces * LANES), lambda g: (0, g)),
        out_shape=jax.ShapeDtypeStruct((tokens, width), jnp.bfloat16),
        scratch_shapes=[pltpu.VMEM((pieces * tokens, rows), jnp.bfloat16)],
        name="unpack",
    )(slot, got)


def exchange(x):
    return lax.all_to_all(x, ("group", "vocab"), split_axis=0, concat_axis=0, tiled=True)


def per_device(shard_ids, row_ids, table, cotangent):
    tokens, width = cotangent.shape
    groups = lax.axis_size("group")
    owners = lax.axis_size("vocab")
    cap = 2 * tokens // owners
    peers = groups * owners
    rows_here, columns = table.shape
    packed, outgoing, slot = pack(
        shard_ids.reshape(1, tokens), row_ids.reshape(1, tokens), cotangent, groups, owners, cap
    )
    arrived = exchange(packed)
    near = lax.all_gather(outgoing, "group", axis=0, tiled=True)
    every = lax.all_gather(near, "vocab", axis=0)
    mine = lax.dynamic_slice_in_dim(every, lax.axis_index("vocab") * cap, cap, axis=2)
    wanted = jnp.moveaxis(mine, 0, 1).reshape(-1)
    picker = (wanted[:, None] == jnp.arange(rows_here, dtype=jnp.int32)[None, :]).astype(jnp.bfloat16)
    found = jnp.dot(picker, table, preferred_element_type=jnp.float32).astype(jnp.bfloat16)
    got = exchange(found.reshape(peers, cap * columns // LANES, LANES))
    table_grad = lax.dot_general(
        picker,
        arrived.reshape(peers * cap, columns),
        (((0,), (0,)), ((), ())),
        preferred_element_type=jnp.float32,
    )
    embeds = unpack(slot, got, groups, width)
    return (embeds, table_grad.astype(jnp.bfloat16))


def solution(mesh):
    in_specs = (
        P(("group", "vocab"), None),
        P(("group", "vocab")),
        P("vocab", "group"),
        P(("group", "vocab"), None),
    )
    out_specs = (P(("group", "vocab"), None), P("vocab", "group"))
    return jax.shard_map(
        per_device, mesh=mesh, in_specs=in_specs, out_specs=out_specs, check_vma=False
    )
```

```python
import functools

import jax
import jax.numpy as jnp
from jax import lax
from jax.experimental import pallas as pl
from jax.experimental.pallas import tpu as pltpu
from jax.sharding import Mesh
from jax.sharding import PartitionSpec as P

LANES = 128


def to_column(row):
    n = row.shape[1]
    here = lax.broadcasted_iota(jnp.int32, (n, n), 0)
    there = lax.broadcasted_iota(jnp.int32, (n, n), 1)
    return jnp.sum(jnp.where(here == there, row, 0), axis=1, keepdims=True)


def pack_kernel(cap, pieces, owners, shard_ref, row_ref, cot_ref, out_ref, ids_ref, slot_ref, hot):
    tokens = shard_ref.shape[1]
    rows = hot.shape[0]

    @pl.when(pl.program_id(0) == 0)
    def _():
        shard = shard_ref[...]
        column = to_column(shard)
        i = lax.broadcasted_iota(jnp.int32, (tokens, tokens), 0)
        j = lax.broadcasted_iota(jnp.int32, (tokens, tokens), 1)
        earlier = jnp.where((column == shard) & (i < j), 1, 0)
        slot = shard * cap + jnp.sum(earlier, axis=0, keepdims=True)
        slot_ref[...] = slot
        target = 2 * lax.broadcasted_iota(jnp.int32, (tokens, owners * cap // 2), 1)
        place, name = to_column(slot), to_column(row_ref[...]) + 1
        named = jnp.where(place == target, name, 0) + jnp.where(place == target + 1, name << 16, 0)
        ids_ref[...] = jnp.sum(named, axis=0, keepdims=True)
        line = lax.broadcasted_iota(jnp.int32, (rows, tokens), 0)
        for c in range(pieces):
            hot[:, c * tokens : (c + 1) * tokens] = jnp.where(
                line == slot * pieces + c, 1.0, 0.0
            ).astype(jnp.bfloat16)

    groups = cot_ref.shape[1] // (pieces * LANES)
    right = []
    for g in range(groups):
        right.append(
            jnp.concatenate(
                [cot_ref[:, (g * pieces + c) * LANES : (g * pieces + c + 1) * LANES] for c in range(pieces)],
                axis=0,
            )
        )
    placed = jnp.dot(hot[...], jnp.concatenate(right, axis=1), preferred_element_type=jnp.float32)
    placed = placed.astype(jnp.bfloat16)
    for g in range(groups):
        block = placed[:, g * LANES : (g + 1) * LANES]
        out_ref[g * owners : (g + 1) * owners] = block.reshape(owners, rows // owners, LANES)


def pack(shard, row, cotangent, groups, owners, cap):
    tokens, width = cotangent.shape
    pieces = width // groups // LANES
    rows = owners * cap * pieces
    step = 2
    return pl.pallas_call(
        functools.partial(pack_kernel, cap, pieces, owners),
        grid=(groups // step,),
        in_specs=[
            pl.BlockSpec((1, tokens), lambda g: (0, 0)),
            pl.BlockSpec((1, tokens), lambda g: (0, 0)),
            pl.BlockSpec((tokens, step * pieces * LANES), lambda g: (0, g)),
        ],
        out_specs=[
            pl.BlockSpec((step * owners, cap * pieces, LANES), lambda g: (g, 0, 0)),
            pl.BlockSpec((1, owners * cap // 2), lambda g: (0, 0)),
            pl.BlockSpec((1, tokens), lambda g: (0, 0)),
        ],
        out_shape=[
            jax.ShapeDtypeStruct((groups * owners, cap * pieces, LANES), jnp.bfloat16),
            jax.ShapeDtypeStruct((1, owners * cap // 2), jnp.int32),
            jax.ShapeDtypeStruct((1, tokens), jnp.int32),
        ],
        scratch_shapes=[pltpu.VMEM((rows, pieces * tokens), jnp.bfloat16)],
        name="pack",
    )(shard, row, cotangent)


def unpack_kernel(pieces, slot_ref, got_ref, out_ref, hot):
    tokens = slot_ref.shape[1]
    rows = hot.shape[1]

    @pl.when(pl.program_id(0) == 0)
    def _():
        slot = to_column(slot_ref[...])
        line = lax.broadcasted_iota(jnp.int32, (tokens, rows), 1)
        for c in range(pieces):
            hot[c * tokens : (c + 1) * tokens, :] = jnp.where(
                line == slot * pieces + c, 1.0, 0.0
            ).astype(jnp.bfloat16)

    groups = out_ref.shape[1] // (pieces * LANES)
    owners = got_ref.shape[0] // groups
    right = [got_ref[g * owners : (g + 1) * owners].reshape(rows, LANES) for g in range(groups)]
    picked = jnp.dot(hot[...], jnp.concatenate(right, axis=1), preferred_element_type=jnp.float32)
    picked = picked.astype(jnp.bfloat16)
    for g in range(groups):
        for c in range(pieces):
            out_ref[:, (g * pieces + c) * LANES : (g * pieces + c + 1) * LANES] = picked[
                c * tokens : (c + 1) * tokens, g * LANES : (g + 1) * LANES
            ]


def unpack(slot, got, groups, width):
    tokens = slot.shape[1]
    pieces = width // groups // LANES
    owners = got.shape[0] // groups
    rows = owners * got.shape[1]
    step = 2
    return pl.pallas_call(
        functools.partial(unpack_kernel, pieces),
        grid=(groups // step,),
        in_specs=[
            pl.BlockSpec((1, tokens), lambda g: (0, 0)),
            pl.BlockSpec((step * owners, got.shape[1], LANES), lambda g: (g, 0, 0)),
        ],
        out_specs=pl.BlockSpec((tokens, step * pieces * LANES), lambda g: (0, g)),
        out_shape=jax.ShapeDtypeStruct((tokens, width), jnp.bfloat16),
        scratch_shapes=[pltpu.VMEM((pieces * tokens, rows), jnp.bfloat16)],
        name="unpack",
    )(slot, got)


def exchange(x):
    return lax.all_to_all(x, ("group", "outer", "inner"), split_axis=0, concat_axis=0, tiled=True)


def per_device(shard_ids, row_ids, table, cotangent):
    tokens, width = cotangent.shape
    groups = lax.axis_size("group")
    owners = lax.axis_size("outer") * lax.axis_size("inner")
    cap = 2 * tokens // owners
    peers = groups * owners
    rows_here, columns = table.shape
    packed, outgoing, slot = pack(
        shard_ids.reshape(1, tokens), row_ids.reshape(1, tokens), cotangent, groups, owners, cap
    )
    arrived = exchange(packed)
    words = lax.all_gather(outgoing, "inner", axis=0, tiled=True)
    words = lax.all_gather(words, "outer", axis=0, tiled=True)
    words = lax.all_gather(words, "group", axis=0, tiled=True)
    here = lax.axis_index("outer") * lax.axis_size("inner") + lax.axis_index("inner")
    mine = lax.dynamic_slice_in_dim(words, here * (cap // 2), cap // 2, axis=1)
    wanted = jnp.stack([mine & 0xFFFF, mine >> 16], axis=2).reshape(-1) - 1
    picker = (wanted[:, None] == jnp.arange(rows_here, dtype=jnp.int32)[None, :]).astype(jnp.bfloat16)
    found = jnp.dot(picker, table, preferred_element_type=jnp.float32).astype(jnp.bfloat16)
    got = exchange(found.reshape(peers, cap * columns // LANES, LANES))
    table_grad = lax.dot_general(
        picker,
        arrived.reshape(peers * cap, columns),
        (((0,), (0,)), ((), ())),
        preferred_element_type=jnp.float32,
    )
    embeds = unpack(slot, got, groups, width)
    return (embeds, table_grad.astype(jnp.bfloat16))


def solution(mesh):
    groups, owners = mesh.shape["group"], mesh.shape["vocab"]
    inner = 1 << (owners.bit_length() - 1) // 2
    grid = Mesh(mesh.devices.reshape(groups, owners // inner, inner), ("group", "outer", "inner"))
    vocab = ("outer", "inner")
    in_specs = (P(("group", *vocab), None), P(("group", *vocab)), P(vocab, "group"), P(("group", *vocab), None))
    out_specs = (P(("group", *vocab), None), P(vocab, "group"))
    return jax.shard_map(
        per_device, mesh=grid, in_specs=in_specs, out_specs=out_specs, check_vma=False
    )
```

```python
import functools

import jax
import jax.numpy as jnp
from jax import lax
from jax.experimental import pallas as pl
from jax.experimental.pallas import tpu as pltpu
from jax.sharding import Mesh
from jax.sharding import PartitionSpec as P

LANES = 128


def to_column(row):
    n = row.shape[1]
    here = lax.broadcasted_iota(jnp.int32, (n, n), 0)
    there = lax.broadcasted_iota(jnp.int32, (n, n), 1)
    return jnp.sum(jnp.where(here == there, row, 0), axis=1, keepdims=True)


def slots_kernel(cap, shard_ref, row_ref, ids_ref, slot_ref):
    tokens = shard_ref.shape[1]
    words = ids_ref.shape[1]
    shard = shard_ref[...]
    i = lax.broadcasted_iota(jnp.int32, (tokens, tokens), 0)
    j = lax.broadcasted_iota(jnp.int32, (tokens, tokens), 1)
    earlier = jnp.where((to_column(shard) == shard) & (i < j), 1, 0)
    slot = shard * cap + jnp.sum(earlier, axis=0, keepdims=True)
    slot_ref[...] = slot
    target = 2 * lax.broadcasted_iota(jnp.int32, (tokens, words), 1)
    place, name = to_column(slot), to_column(row_ref[...]) + 1
    named = jnp.where(place == target, name, 0) + jnp.where(place == target + 1, name << 16, 0)
    ids_ref[...] = jnp.sum(named, axis=0, keepdims=True)


def slots(shard, row, owners, cap):
    return pl.pallas_call(
        functools.partial(slots_kernel, cap),
        out_shape=[
            jax.ShapeDtypeStruct((1, owners * cap // 2), jnp.int32),
            jax.ShapeDtypeStruct(shard.shape, jnp.int32),
        ],
        name="slots",
    )(shard, row)


def pack_kernel(pieces, owners, slot_ref, cot_ref, out_ref, hot):
    tokens = slot_ref.shape[1]
    rows = hot.shape[0]

    @pl.when(pl.program_id(0) == 0)
    def _():
        line = lax.broadcasted_iota(jnp.int32, (rows, tokens), 0)
        for c in range(pieces):
            hot[:, c * tokens : (c + 1) * tokens] = jnp.where(
                line == slot_ref[...] * pieces + c, 1.0, 0.0
            ).astype(jnp.bfloat16)

    groups = cot_ref.shape[1] // (pieces * LANES)
    right = []
    for g in range(groups):
        right.append(
            jnp.concatenate(
                [cot_ref[:, (g * pieces + c) * LANES : (g * pieces + c + 1) * LANES] for c in range(pieces)],
                axis=0,
            )
        )
    placed = jnp.dot(hot[...], jnp.concatenate(right, axis=1), preferred_element_type=jnp.float32)
    placed = placed.astype(jnp.bfloat16)
    for g in range(groups):
        block = placed[:, g * LANES : (g + 1) * LANES]
        out_ref[g * owners : (g + 1) * owners] = block.reshape(owners, rows // owners, LANES)


def pack(slot, cotangent, groups, owners, cap):
    tokens, width = cotangent.shape
    pieces = width // groups // LANES
    rows = owners * cap * pieces
    step = 2
    return pl.pallas_call(
        functools.partial(pack_kernel, pieces, owners),
        grid=(groups // step,),
        in_specs=[
            pl.BlockSpec((1, tokens), lambda g: (0, 0)),
            pl.BlockSpec((tokens, step * pieces * LANES), lambda g: (0, g)),
        ],
        out_specs=pl.BlockSpec((step * owners, cap * pieces, LANES), lambda g: (g, 0, 0)),
        out_shape=jax.ShapeDtypeStruct((groups * owners, cap * pieces, LANES), jnp.bfloat16),
        scratch_shapes=[pltpu.VMEM((rows, pieces * tokens), jnp.bfloat16)],
        cost_estimate=pl.CostEstimate(
            flops=2 * rows * pieces * tokens * groups * LANES,
            bytes_accessed=2 * (tokens * width + groups * rows * LANES),
            transcendentals=0,
        ),
        name="pack",
    )(slot, cotangent)


def pick_kernel(inner, here_ref, below_ref, near_ref, above_ref, out_ref):
    outer_at, inner_at = here_ref[0], here_ref[1]
    rows = jnp.concatenate([below_ref[inner:, :], near_ref[...], above_ref[...]], axis=0)
    owners, lanes = rows.shape
    each = lanes // owners
    lane = lax.broadcasted_iota(jnp.int32, (owners, lanes), 1)
    line = lax.broadcasted_iota(jnp.int32, (owners, lanes), 0)
    far = lax.rem(outer_at + line // inner + owners // inner - 3, owners // inner)
    close = lax.rem(inner_at + lax.rem(line, inner) + inner - 3, inner)
    device = far * inner + close
    out = jnp.zeros((owners, lanes), jnp.int32)
    for w in range(each):
        mine = jnp.where(lane == (outer_at * inner + inner_at) * each + w, rows, 0)
        out = out + jnp.where(lane == w * owners + device, jnp.sum(mine, axis=1, keepdims=True), 0)
    out_ref[...] = jnp.sum(out, axis=0, keepdims=True)


def pick(here, below, near, above, inner):
    return pl.pallas_call(
        functools.partial(pick_kernel, inner),
        in_specs=[pl.BlockSpec(memory_space=pltpu.SMEM)] + [pl.BlockSpec(memory_space=pltpu.VMEM)] * 3,
        out_specs=pl.BlockSpec(memory_space=pltpu.VMEM),
        out_shape=jax.ShapeDtypeStruct((1, near.shape[1]), jnp.int32),
        name="pick",
    )(here, below, near, above)


def lookup_kernel(cap, words_ref, table_ref, out_ref, lines):
    groups = words_ref.shape[0]
    devices = out_ref.shape[0]
    rows, columns = table_ref.shape
    owners = devices // groups
    pieces = columns // LANES
    here = lax.broadcasted_iota(jnp.int32, (owners, cap // 2 * owners), 0)
    there = lax.broadcasted_iota(jnp.int32, (owners, cap // 2 * owners), 1)
    row = lax.broadcasted_iota(jnp.int32, (devices, rows), 1) + 1
    for w in range(cap // 2):
        word = jnp.concatenate(
            [
                jnp.sum(jnp.where(there == here + w * owners, words_ref[g], 0), axis=1, keepdims=True)
                for g in range(groups)
            ],
            axis=0,
        )
        for half in range(2):
            name = word >> 16 if half else word & 0xFFFF
            hot = jnp.where(name == row, 1.0, 0.0).astype(jnp.bfloat16)
            found = jnp.dot(hot, table_ref[...], preferred_element_type=jnp.float32)
            for c in range(pieces):
                line = (2 * w + half) * pieces + c
                lines[pl.ds(line, devices, stride=cap * pieces), :] = found[:, c * LANES : (c + 1) * LANES]
    out_ref[...] = lines[...].astype(jnp.bfloat16).reshape(out_ref.shape)


def lookup(words, table, owners, cap):
    groups = words.shape[0]
    rows, columns = table.shape
    pieces = columns // LANES
    step = 2
    return pl.pallas_call(
        functools.partial(lookup_kernel, cap),
        grid=(groups // step,),
        in_specs=[
            pl.BlockSpec((step, 1, words.shape[2]), lambda g: (g, 0, 0)),
            pl.BlockSpec((rows, columns), lambda g: (0, 0)),
        ],
        out_specs=pl.BlockSpec((step * owners, cap * pieces, LANES), lambda g: (g, 0, 0)),
        out_shape=jax.ShapeDtypeStruct((groups * owners, cap * pieces, LANES), jnp.bfloat16),
        scratch_shapes=[pltpu.VMEM((step * owners * cap * pieces, LANES), jnp.float32)],
        cost_estimate=pl.CostEstimate(
            flops=2 * groups * owners * cap * rows * columns,
            bytes_accessed=2 * (rows * columns + groups * owners * cap * columns),
            transcendentals=0,
        ),
        name="lookup",
    )(words, table)


def shifted(x, axis, offset):
    size = lax.axis_size(axis)
    return lax.ppermute(x, axis, [(i, (i - offset) % size) for i in range(size)])


def neighbours(x, axis):
    near = jnp.concatenate([shifted(x, axis, -1), x, shifted(x, axis, 1)], axis=0)
    return shifted(near, axis, -3), near, shifted(near, axis, 3)


def unpack_kernel(pieces, slot_ref, got_ref, out_ref, hot):
    tokens = slot_ref.shape[1]
    rows = hot.shape[1]

    @pl.when(pl.program_id(0) == 0)
    def _():
        slot = to_column(slot_ref[...])
        line = lax.broadcasted_iota(jnp.int32, (tokens, rows), 1)
        for c in range(pieces):
            hot[c * tokens : (c + 1) * tokens, :] = jnp.where(
                line == slot * pieces + c, 1.0, 0.0
            ).astype(jnp.bfloat16)

    groups = out_ref.shape[1] // (pieces * LANES)
    owners = got_ref.shape[0] // groups
    right = [got_ref[g * owners : (g + 1) * owners].reshape(rows, LANES) for g in range(groups)]
    picked = jnp.dot(hot[...], jnp.concatenate(right, axis=1), preferred_element_type=jnp.float32)
    picked = picked.astype(jnp.bfloat16)
    for g in range(groups):
        for c in range(pieces):
            out_ref[:, (g * pieces + c) * LANES : (g * pieces + c + 1) * LANES] = picked[
                c * tokens : (c + 1) * tokens, g * LANES : (g + 1) * LANES
            ]


def unpack(slot, got, groups, width):
    tokens = slot.shape[1]
    pieces = width // groups // LANES
    owners = got.shape[0] // groups
    rows = owners * got.shape[1]
    step = 2
    return pl.pallas_call(
        functools.partial(unpack_kernel, pieces),
        grid=(groups // step,),
        in_specs=[
            pl.BlockSpec((1, tokens), lambda g: (0, 0)),
            pl.BlockSpec((step * owners, got.shape[1], LANES), lambda g: (g, 0, 0)),
        ],
        out_specs=pl.BlockSpec((tokens, step * pieces * LANES), lambda g: (0, g)),
        out_shape=jax.ShapeDtypeStruct((tokens, width), jnp.bfloat16),
        scratch_shapes=[pltpu.VMEM((pieces * tokens, rows), jnp.bfloat16)],
        name="unpack",
    )(slot, got)


def exchange(x):
    return lax.all_to_all(x, ("group", "outer", "inner"), split_axis=0, concat_axis=0, tiled=True)


def per_device(shard_ids, row_ids, table, cotangent):
    tokens, width = cotangent.shape
    groups = lax.axis_size("group")
    owners = lax.axis_size("outer") * lax.axis_size("inner")
    cap = 2 * tokens // owners
    peers = groups * owners
    rows_here, columns = table.shape
    outgoing, slot = slots(shard_ids.reshape(1, tokens), row_ids.reshape(1, tokens), owners, cap)
    below, near, above = neighbours(outgoing, "inner")
    packed = pack(slot, cotangent, groups, owners, cap)
    line, packed = lax.optimization_barrier((jnp.concatenate([below[1:], near, above], axis=0), packed))
    arrived = exchange(packed)
    below, near, above = neighbours(line, "outer")
    here = jnp.stack([lax.axis_index("outer"), lax.axis_index("inner")]).astype(jnp.int32)
    mine = pick(here, below, near, above, lax.axis_size("inner"))
    words = lax.all_gather(mine, "group", axis=0)
    got = exchange(lookup(words, table, owners, cap))
    words = words.reshape(groups, cap // 2, owners)
    wanted = jnp.stack([words & 0xFFFF, words >> 16], axis=2).reshape(groups, cap, owners)
    wanted = jnp.swapaxes(wanted, 1, 2).reshape(-1) - 1
    picker = (wanted[:, None] == jnp.arange(rows_here, dtype=jnp.int32)[None, :]).astype(jnp.bfloat16)
    table_grad = lax.dot_general(
        picker,
        arrived.reshape(peers * cap, columns),
        (((0,), (0,)), ((), ())),
        preferred_element_type=jnp.float32,
    )
    embeds = unpack(slot, got, groups, width)
    return (embeds, table_grad.astype(jnp.bfloat16))


def solution(mesh):
    groups, owners = mesh.shape["group"], mesh.shape["vocab"]
    inner = 8
    grid = Mesh(mesh.devices.reshape(groups, owners // inner, inner), ("group", "outer", "inner"))
    vocab = ("outer", "inner")
    in_specs = (P(("group", *vocab), None), P(("group", *vocab)), P(vocab, "group"), P(("group", *vocab), None))
    out_specs = (P(("group", *vocab), None), P(vocab, "group"))
    return jax.shard_map(
        per_device, mesh=grid, in_specs=in_specs, out_specs=out_specs, check_vma=False
    )
```

```python
import functools

import jax
import jax.numpy as jnp
from jax import lax
from jax.experimental import pallas as pl
from jax.experimental.pallas import tpu as pltpu
from jax.sharding import PartitionSpec as P

LANES = 128


def to_column(row):
    n = row.shape[1]
    here = lax.broadcasted_iota(jnp.int32, (n, n), 0)
    there = lax.broadcasted_iota(jnp.int32, (n, n), 1)
    return jnp.sum(jnp.where(here == there, row, 0), axis=1, keepdims=True)


def slots_kernel(cap, shard_ref, row_ref, ids_ref, slot_ref):
    tokens = shard_ref.shape[1]
    owners = ids_ref.shape[0]
    shard = shard_ref[...]
    i = lax.broadcasted_iota(jnp.int32, (tokens, tokens), 0)
    j = lax.broadcasted_iota(jnp.int32, (tokens, tokens), 1)
    earlier = jnp.where((to_column(shard) == shard) & (i < j), 1, 0)
    slot = shard * cap + jnp.sum(earlier, axis=0, keepdims=True)
    slot_ref[...] = slot
    first = cap * lax.broadcasted_iota(jnp.int32, (owners, tokens), 0)
    lane = lax.broadcasted_iota(jnp.int32, (owners, LANES), 1)
    name = row_ref[...] + 1
    ids = jnp.zeros((owners, LANES), jnp.int32)
    for w in range(cap // 2):
        named = jnp.where(slot == first + 2 * w, name, 0) + jnp.where(slot == first + 2 * w + 1, name << 16, 0)
        ids = jnp.where(lane == w, jnp.sum(named, axis=1, keepdims=True), ids)
    ids_ref[...] = ids


def slots(shard, row, owners, cap):
    return pl.pallas_call(
        functools.partial(slots_kernel, cap),
        out_shape=[
            jax.ShapeDtypeStruct((owners, LANES), jnp.int32),
            jax.ShapeDtypeStruct(shard.shape, jnp.int32),
        ],
        name="slots",
    )(shard, row)


def pack_kernel(pieces, owners, slot_ref, cot_ref, out_ref, hot):
    tokens = slot_ref.shape[1]
    rows = hot.shape[0]

    @pl.when(pl.program_id(0) == 0)
    def _():
        line = lax.broadcasted_iota(jnp.int32, (rows, tokens), 0)
        for c in range(pieces):
            hot[:, c * tokens : (c + 1) * tokens] = jnp.where(
                line == slot_ref[...] * pieces + c, 1.0, 0.0
            ).astype(jnp.bfloat16)

    groups = cot_ref.shape[1] // (pieces * LANES)
    right = []
    for g in range(groups):
        right.append(
            jnp.concatenate(
                [cot_ref[:, (g * pieces + c) * LANES : (g * pieces + c + 1) * LANES] for c in range(pieces)],
                axis=0,
            )
        )
    placed = jnp.dot(hot[...], jnp.concatenate(right, axis=1), preferred_element_type=jnp.float32)
    placed = placed.astype(jnp.bfloat16)
    for g in range(groups):
        block = placed[:, g * LANES : (g + 1) * LANES]
        out_ref[g * owners : (g + 1) * owners] = block.reshape(owners, rows // owners, LANES)


def pack(slot, cotangent, groups, owners, cap):
    tokens, width = cotangent.shape
    pieces = width // groups // LANES
    rows = owners * cap * pieces
    step = 2
    return pl.pallas_call(
        functools.partial(pack_kernel, pieces, owners),
        grid=(groups // step,),
        in_specs=[
            pl.BlockSpec((1, tokens), lambda g: (0, 0)),
            pl.BlockSpec((tokens, step * pieces * LANES), lambda g: (0, g)),
        ],
        out_specs=pl.BlockSpec((step * owners, cap * pieces, LANES), lambda g: (g, 0, 0)),
        out_shape=jax.ShapeDtypeStruct((groups * owners, cap * pieces, LANES), jnp.bfloat16),
        scratch_shapes=[pltpu.VMEM((rows, pieces * tokens), jnp.bfloat16)],
        cost_estimate=pl.CostEstimate(
            flops=2 * rows * pieces * tokens * groups * LANES,
            bytes_accessed=2 * (tokens * width + groups * rows * LANES),
            transcendentals=0,
        ),
        name="pack",
    )(slot, cotangent)


def pick_kernel(ids_ref, out_ref):
    ids = ids_ref[...]
    owners, lanes = ids.shape
    lane = lax.broadcasted_iota(jnp.int32, (owners, lanes), 1)
    line = lax.broadcasted_iota(jnp.int32, (owners, lanes), 0)
    out = jnp.zeros((owners, lanes), jnp.int32)
    for w in range(out_ref.shape[1] // owners):
        word = jnp.sum(jnp.where(lane == w, ids, 0), axis=1, keepdims=True)
        out = jnp.where(lane == w * owners + line, word, out)
    out_ref[...] = jnp.sum(out, axis=0, keepdims=True)


def pick(ids, cap):
    owners = ids.shape[0]
    return pl.pallas_call(
        pick_kernel,
        out_shape=jax.ShapeDtypeStruct((1, cap // 2 * owners), jnp.int32),
        name="pick",
    )(ids)


def lookup_kernel(cap, words_ref, table_ref, out_ref, lines):
    groups = words_ref.shape[0]
    devices = out_ref.shape[0]
    rows, columns = table_ref.shape
    owners = devices // groups
    pieces = columns // LANES
    here = lax.broadcasted_iota(jnp.int32, (owners, cap // 2 * owners), 0)
    there = lax.broadcasted_iota(jnp.int32, (owners, cap // 2 * owners), 1)
    row = lax.broadcasted_iota(jnp.int32, (devices, rows), 1) + 1
    for w in range(cap // 2):
        word = jnp.concatenate(
            [
                jnp.sum(jnp.where(there == here + w * owners, words_ref[g], 0), axis=1, keepdims=True)
                for g in range(groups)
            ],
            axis=0,
        )
        for half in range(2):
            name = word >> 16 if half else word & 0xFFFF
            hot = jnp.where(name == row, 1.0, 0.0).astype(jnp.bfloat16)
            found = jnp.dot(hot, table_ref[...], preferred_element_type=jnp.float32)
            for c in range(pieces):
                line = (2 * w + half) * pieces + c
                lines[pl.ds(line, devices, stride=cap * pieces), :] = found[:, c * LANES : (c + 1) * LANES]
    out_ref[...] = lines[...].astype(jnp.bfloat16).reshape(out_ref.shape)


def lookup(words, table, owners, cap):
    groups = words.shape[0]
    rows, columns = table.shape
    pieces = columns // LANES
    step = 2
    return pl.pallas_call(
        functools.partial(lookup_kernel, cap),
        grid=(groups // step,),
        in_specs=[
            pl.BlockSpec((step, 1, words.shape[2]), lambda g: (g, 0, 0)),
            pl.BlockSpec((rows, columns), lambda g: (0, 0)),
        ],
        out_specs=pl.BlockSpec((step * owners, cap * pieces, LANES), lambda g: (g, 0, 0)),
        out_shape=jax.ShapeDtypeStruct((groups * owners, cap * pieces, LANES), jnp.bfloat16),
        scratch_shapes=[pltpu.VMEM((step * owners * cap * pieces, LANES), jnp.float32)],
        cost_estimate=pl.CostEstimate(
            flops=2 * groups * owners * cap * rows * columns,
            bytes_accessed=2 * (rows * columns + groups * owners * cap * columns),
            transcendentals=0,
        ),
        name="lookup",
    )(words, table)


def shifted(x, axis, offset):
    size = lax.axis_size(axis)
    return lax.ppermute(x, axis, [(i, (i - offset) % size) for i in range(size)])


def neighbours(x, axis):
    near = jnp.concatenate([shifted(x, axis, -1), x, shifted(x, axis, 1)], axis=0)
    return shifted(near, axis, -3), near, shifted(near, axis, 3)


def unpack_kernel(pieces, slot_ref, got_ref, out_ref, hot):
    tokens = slot_ref.shape[1]
    rows = hot.shape[1]

    @pl.when(pl.program_id(0) == 0)
    def _():
        slot = to_column(slot_ref[...])
        line = lax.broadcasted_iota(jnp.int32, (tokens, rows), 1)
        for c in range(pieces):
            hot[c * tokens : (c + 1) * tokens, :] = jnp.where(
                line == slot * pieces + c, 1.0, 0.0
            ).astype(jnp.bfloat16)

    groups = out_ref.shape[1] // (pieces * LANES)
    owners = got_ref.shape[0] // groups
    right = [got_ref[g * owners : (g + 1) * owners].reshape(rows, LANES) for g in range(groups)]
    picked = jnp.dot(hot[...], jnp.concatenate(right, axis=1), preferred_element_type=jnp.float32)
    picked = picked.astype(jnp.bfloat16)
    for g in range(groups):
        for c in range(pieces):
            out_ref[:, (g * pieces + c) * LANES : (g * pieces + c + 1) * LANES] = picked[
                c * tokens : (c + 1) * tokens, g * LANES : (g + 1) * LANES
            ]


def unpack(slot, got, groups, width):
    tokens = slot.shape[1]
    pieces = width // groups // LANES
    owners = got.shape[0] // groups
    rows = owners * got.shape[1]
    step = 2
    return pl.pallas_call(
        functools.partial(unpack_kernel, pieces),
        grid=(groups // step,),
        in_specs=[
            pl.BlockSpec((1, tokens), lambda g: (0, 0)),
            pl.BlockSpec((step * owners, got.shape[1], LANES), lambda g: (g, 0, 0)),
        ],
        out_specs=pl.BlockSpec((tokens, step * pieces * LANES), lambda g: (0, g)),
        out_shape=jax.ShapeDtypeStruct((tokens, width), jnp.bfloat16),
        scratch_shapes=[pltpu.VMEM((pieces * tokens, rows), jnp.bfloat16)],
        name="unpack",
    )(slot, got)


def exchange(x, axes):
    return lax.all_to_all(x, axes, split_axis=0, concat_axis=0, tiled=True)


def per_device(shard_ids, row_ids, table, cotangent):
    tokens, width = cotangent.shape
    groups = lax.axis_size("group")
    owners = lax.axis_size("vocab")
    cap = 2 * tokens // owners
    peers = groups * owners
    rows_here, columns = table.shape
    outgoing, slot = slots(shard_ids.reshape(1, tokens), row_ids.reshape(1, tokens), owners, cap)
    ids = exchange(outgoing.reshape(owners, 1, LANES), "vocab")
    packed = pack(slot, cotangent, groups, owners, cap)
    ids, packed = lax.optimization_barrier((ids, packed))
    arrived = exchange(packed, ("group", "vocab"))
    words = lax.all_gather(pick(ids.reshape(owners, LANES), cap), "group", axis=0)
    got = exchange(lookup(words, table, owners, cap), ("group", "vocab"))
    words = words.reshape(groups, cap // 2, owners)
    wanted = jnp.stack([words & 0xFFFF, words >> 16], axis=2).reshape(groups, cap, owners)
    wanted = jnp.swapaxes(wanted, 1, 2).reshape(-1) - 1
    picker = (wanted[:, None] == jnp.arange(rows_here, dtype=jnp.int32)[None, :]).astype(jnp.bfloat16)
    table_grad = lax.dot_general(
        picker,
        arrived.reshape(peers * cap, columns),
        (((0,), (0,)), ((), ())),
        preferred_element_type=jnp.float32,
    )
    embeds = unpack(slot, got, groups, width)
    return (embeds, table_grad.astype(jnp.bfloat16))


def solution(mesh):
    in_specs = (
        P(("group", "vocab"), None),
        P(("group", "vocab")),
        P("vocab", "group"),
        P(("group", "vocab"), None),
    )
    out_specs = (P(("group", "vocab"), None), P("vocab", "group"))
    return jax.shard_map(
        per_device, mesh=mesh, in_specs=in_specs, out_specs=out_specs, check_vma=False
    )
```

```python
import functools

import jax
import jax.numpy as jnp
from jax import lax
from jax.experimental import pallas as pl
from jax.experimental.pallas import tpu as pltpu
from jax.sharding import PartitionSpec as P

LANES = 128
EXTRA = 8
VMEM = pl.BlockSpec(memory_space=pltpu.VMEM)
SMEM = pl.BlockSpec(memory_space=pltpu.SMEM)


def to_column(row):
    n = row.shape[1]
    here = lax.broadcasted_iota(jnp.int32, (n, n), 0)
    there = lax.broadcasted_iota(jnp.int32, (n, n), 1)
    return jnp.sum(jnp.where(here == there, row, 0), axis=1, keepdims=True)


def slots_kernel(cap, shard_ref, row_ref, ids_ref, slot_ref):
    tokens = shard_ref.shape[1]
    groups, owners, _ = ids_ref.shape
    shard = shard_ref[...]
    i = lax.broadcasted_iota(jnp.int32, (tokens, tokens), 0)
    j = lax.broadcasted_iota(jnp.int32, (tokens, tokens), 1)
    earlier = jnp.where((to_column(shard) == shard) & (i < j), 1, 0)
    slot = shard * cap + jnp.sum(earlier, axis=0, keepdims=True)
    slot_ref[...] = slot
    first = cap * lax.broadcasted_iota(jnp.int32, (owners, tokens), 0)
    lane = lax.broadcasted_iota(jnp.int32, (owners, LANES), 1)
    name = row_ref[...] + 1
    ids = jnp.zeros((owners, LANES), jnp.int32)
    for w in range(cap // 2):
        named = jnp.where(slot == first + 2 * w, name, 0) + jnp.where(slot == first + 2 * w + 1, name << 16, 0)
        ids = jnp.where(lane == w, jnp.sum(named, axis=1, keepdims=True), ids)
    for g in range(groups):
        ids_ref[g] = ids


def slots(shard, row, groups, owners, cap):
    return pl.pallas_call(
        functools.partial(slots_kernel, cap),
        out_shape=[
            jax.ShapeDtypeStruct((groups, owners, LANES), jnp.int32),
            jax.ShapeDtypeStruct(shard.shape, jnp.int32),
        ],
        name="slots",
    )(shard, row)


def lookup_kernel(cap, me_ref, ids_ref, table_ref, out_ref, lines_ref):
    groups, owners, _ = ids_ref.shape
    rows = table_ref.shape[0]
    lane = lax.broadcasted_iota(jnp.int32, (owners, LANES), 1)
    for d in range(groups):
        ids = ids_ref[lax.rem(me_ref[0] + groups - d, groups)]
        for w in range(cap // 2):
            word = jnp.sum(jnp.where(lane == w, ids, 0), axis=1, keepdims=True)
            word = jnp.broadcast_to(word, (owners, LANES))
            at = d * cap + 2 * w
            lines_ref[pl.ds(at, owners, stride=groups * cap), :] = word & 0xFFFF
            lines_ref[pl.ds(at + 1, owners, stride=groups * cap), :] = word >> 16
    chunk = 256
    row = lax.broadcasted_iota(jnp.int32, (chunk, rows), 1) + 1
    for m in range(0, out_ref.shape[0], chunk):
        hot = jnp.where(lines_ref[m : m + chunk, :1] == row, 1.0, 0.0).astype(jnp.bfloat16)
        found = jnp.dot(hot, table_ref[...], preferred_element_type=jnp.float32)
        out_ref[m : m + chunk] = found.astype(jnp.bfloat16)


def lookup(me, ids, table, cap):
    groups, owners, _ = ids.shape
    count = groups * owners * cap
    return pl.pallas_call(
        functools.partial(lookup_kernel, cap),
        in_specs=[SMEM, VMEM, VMEM],
        out_specs=[VMEM, VMEM],
        out_shape=[
            jax.ShapeDtypeStruct((count, table.shape[1]), jnp.bfloat16),
            jax.ShapeDtypeStruct((count, LANES), jnp.int32),
        ],
        name="lookup",
    )(me, ids, table)


def cut_kernel(me_ref, slot_ref, cot_ref, *out_refs):
    groups = len(out_refs)
    tokens, width = cot_ref.shape
    columns = width // groups
    slot = jnp.broadcast_to(slot_ref[...].astype(jnp.float32), (EXTRA, tokens)).astype(jnp.bfloat16)
    for d, out_ref in enumerate(out_refs):
        at = pl.multiple_of(lax.rem(me_ref[0] + d, groups) * columns, columns)
        out_ref[:tokens, :] = cot_ref[:, pl.ds(at, columns)]
        out_ref[tokens:, :] = jnp.concatenate([slot] * (columns // tokens), axis=1)


def cut(me, slot, cotangent, groups):
    tokens, width = cotangent.shape
    piece = jax.ShapeDtypeStruct((tokens + EXTRA, width // groups), jnp.bfloat16)
    return pl.pallas_call(
        cut_kernel,
        in_specs=[SMEM, VMEM, VMEM],
        out_specs=[VMEM] * groups,
        out_shape=[piece] * groups,
        name="cut",
    )(me, slot, cotangent)


def target_line(slot, cap, part, parts):
    return lax.div(slot, cap) * (parts * cap) + part * cap + lax.rem(slot, cap)


def slots_of(piece_ref):
    tokens = piece_ref.shape[0] - EXTRA
    return piece_ref[tokens:, :tokens].astype(jnp.float32)[:1].astype(jnp.int32)


def pack_kernel(cap, *refs):
    piece_refs, out_ref = refs[:-1], refs[-1]
    groups = len(piece_refs)
    owners = out_ref.shape[0]
    tokens = piece_refs[0].shape[0] - EXTRA
    columns = out_ref.shape[2]
    parts = groups // 2
    line = lax.broadcasted_iota(jnp.int32, (owners * parts * cap, tokens), 0)
    for half in range(2):
        group = piece_refs[half * parts : (half + 1) * parts]
        hot = jnp.concatenate(
            [
                jnp.where(line == target_line(slots_of(ref), cap, part, parts), 1.0, 0.0).astype(jnp.bfloat16)
                for part, ref in enumerate(group)
            ],
            axis=1,
        )
        right = jnp.concatenate([ref[:tokens, :] for ref in group], axis=0)
        placed = jnp.dot(hot, right, preferred_element_type=jnp.float32).astype(jnp.bfloat16)
        out_ref[:, half * parts * cap : (half + 1) * parts * cap, :] = placed.reshape(owners, parts * cap, columns)


def pack(pieces, owners, cap):
    groups = len(pieces)
    return pl.pallas_call(
        functools.partial(pack_kernel, cap),
        in_specs=[VMEM] * groups,
        out_specs=VMEM,
        out_shape=jax.ShapeDtypeStruct((owners, groups * cap, pieces[0].shape[1]), jnp.bfloat16),
        name="pack",
    )(*pieces)


def unpack_kernel(cap, groups, *refs):
    piece_refs, got_ref, out_refs = refs[:groups], refs[groups], refs[groups + 1 :]
    owners, _, columns = got_ref.shape
    tokens = out_refs[0].shape[0]
    parts = groups // 2
    line = lax.broadcasted_iota(jnp.int32, (tokens, owners * parts * cap), 1)
    for half in range(2):
        group = piece_refs[half * parts : (half + 1) * parts]
        hot = jnp.concatenate(
            [
                jnp.where(
                    line == to_column(target_line(slots_of(ref), cap, part, parts)), 1.0, 0.0
                ).astype(jnp.bfloat16)
                for part, ref in enumerate(group)
            ],
            axis=0,
        )
        right = got_ref[:, half * parts * cap : (half + 1) * parts * cap, :].reshape(-1, columns)
        picked = jnp.dot(hot, right, preferred_element_type=jnp.float32).astype(jnp.bfloat16)
        for part in range(parts):
            out_refs[half * parts + part][...] = picked[part * tokens : (part + 1) * tokens]


def unpack(pieces, got, cap):
    groups = len(pieces)
    tokens = pieces[0].shape[0] - EXTRA
    return pl.pallas_call(
        functools.partial(unpack_kernel, cap, groups),
        in_specs=[VMEM] * (groups + 1),
        out_specs=[VMEM] * groups,
        out_shape=[jax.ShapeDtypeStruct((tokens, got.shape[2]), jnp.bfloat16)] * groups,
        name="unpack",
    )(*pieces, got)


def join_kernel(me_ref, *refs):
    out_ref = refs[-1]
    groups = len(refs) - 1
    for d, ref in enumerate(refs[:-1]):
        columns = ref.shape[1]
        at = pl.multiple_of(lax.rem(me_ref[0] + d, groups) * columns, columns)
        out_ref[:, pl.ds(at, columns)] = ref[...]


def join(me, pieces):
    tokens, columns = pieces[0].shape
    return pl.pallas_call(
        join_kernel,
        in_specs=[SMEM] + [VMEM] * len(pieces),
        out_specs=VMEM,
        out_shape=jax.ShapeDtypeStruct((tokens, columns * len(pieces)), jnp.bfloat16),
        name="join",
    )(me, *pieces)


def exchange(x, axes):
    return lax.all_to_all(x, axes, split_axis=0, concat_axis=0, tiled=True)


def pass_on(pieces, sign):
    size = len(pieces)
    moved = [lax.ppermute(pieces[d], "group", [(i, (i + sign * d) % size) for i in range(size)]) for d in range(1, size)]
    return [pieces[0], *moved]


def per_device(shard_ids, row_ids, table, cotangent):
    tokens, width = cotangent.shape
    groups = lax.axis_size("group")
    owners = lax.axis_size("vocab")
    cap = 2 * tokens // owners
    rows_here, columns = table.shape
    me = lax.axis_index("group").astype(jnp.int32).reshape(1)
    ids, slot = slots(shard_ids.reshape(1, tokens), row_ids.reshape(1, tokens), groups, owners, cap)
    ids = exchange(ids.reshape(groups * owners, 1, LANES), ("group", "vocab"))
    pieces = cut(me, slot, cotangent, groups)
    found, lines = lookup(me, ids.reshape(groups, owners, LANES), table, cap)
    found, pieces = lax.optimization_barrier((found, pieces))
    got = exchange(found.reshape(owners, groups * cap, columns), "vocab")
    pieces = pass_on(pieces, 1)
    packed = pack(pieces, owners, cap)
    got, packed = lax.optimization_barrier((got, packed))
    arrived = exchange(packed, "vocab")
    embeds = join(me, pass_on(unpack(pieces, got, cap), -1))
    wanted = lines[:, 0] - 1
    picker = (wanted[:, None] == jnp.arange(rows_here, dtype=jnp.int32)[None, :]).astype(jnp.bfloat16)
    table_grad = lax.dot_general(
        picker, arrived.reshape(-1, columns), (((0,), (0,)), ((), ())), preferred_element_type=jnp.float32
    )
    return (embeds, table_grad.astype(jnp.bfloat16))


def solution(mesh):
    in_specs = (
        P(("group", "vocab"), None),
        P(("group", "vocab")),
        P("vocab", "group"),
        P(("group", "vocab"), None),
    )
    out_specs = (P(("group", "vocab"), None), P("vocab", "group"))
    return jax.shard_map(
        per_device, mesh=mesh, in_specs=in_specs, out_specs=out_specs, check_vma=False
    )
```

```python
import functools

import jax
import jax.numpy as jnp
from jax import lax
from jax.experimental import pallas as pl
from jax.experimental.pallas import tpu as pltpu
from jax.sharding import PartitionSpec as P

LANES = 128
EXTRA = 8
VMEM = pl.BlockSpec(memory_space=pltpu.VMEM)
SMEM = pl.BlockSpec(memory_space=pltpu.SMEM)


def to_column(row):
    n = row.shape[1]
    here = lax.broadcasted_iota(jnp.int32, (n, n), 0)
    there = lax.broadcasted_iota(jnp.int32, (n, n), 1)
    return jnp.sum(jnp.where(here == there, row, 0), axis=1, keepdims=True)


def slots_kernel(cap, shard_ref, row_ref, ids_ref, slot_ref):
    tokens = shard_ref.shape[1]
    owners = ids_ref.shape[0]
    shard = shard_ref[...]
    i = lax.broadcasted_iota(jnp.int32, (tokens, tokens), 0)
    j = lax.broadcasted_iota(jnp.int32, (tokens, tokens), 1)
    earlier = jnp.where((to_column(shard) == shard) & (i < j), 1, 0)
    slot = shard * cap + jnp.sum(earlier, axis=0, keepdims=True)
    slot_ref[...] = slot
    first = cap * lax.broadcasted_iota(jnp.int32, (owners, tokens), 0)
    lane = lax.broadcasted_iota(jnp.int32, (owners, LANES), 1)
    name = row_ref[...] + 1
    ids = jnp.zeros((owners, LANES), jnp.int32)
    for w in range(cap // 2):
        named = jnp.where(slot == first + 2 * w, name, 0) + jnp.where(slot == first + 2 * w + 1, name << 16, 0)
        ids = jnp.where(lane == w, jnp.sum(named, axis=1, keepdims=True), ids)
    ids_ref[...] = ids


def slots(shard, row, owners, cap):
    return pl.pallas_call(
        functools.partial(slots_kernel, cap),
        out_shape=[
            jax.ShapeDtypeStruct((owners, LANES), jnp.int32),
            jax.ShapeDtypeStruct(shard.shape, jnp.int32),
        ],
        name="slots",
    )(shard, row)


def lookup_kernel(cap, me_ref, ids_ref, table_ref, out_ref, names_ref, lines_ref):
    groups, owners, _ = ids_ref.shape
    rows = table_ref.shape[0]
    chunk = out_ref.shape[0]

    @pl.when(pl.program_id(0) == 0)
    def _():
        lane = lax.broadcasted_iota(jnp.int32, (owners, LANES), 1)
        for d in range(groups):
            ids = ids_ref[lax.rem(me_ref[0] + groups - d, groups)]
            for w in range(cap // 2):
                word = jnp.sum(jnp.where(lane == w, ids, 0), axis=1, keepdims=True)
                word = jnp.broadcast_to(word, (owners, LANES))
                at = d * cap + 2 * w
                lines_ref[pl.ds(at, owners, stride=groups * cap), :] = word & 0xFFFF
                lines_ref[pl.ds(at + 1, owners, stride=groups * cap), :] = word >> 16

    names = lines_ref[pl.ds(pl.multiple_of(pl.program_id(0) * chunk, chunk), chunk), :]
    names_ref[...] = names
    row = lax.broadcasted_iota(jnp.int32, (chunk, rows), 1) + 1
    hot = jnp.where(names[:, :1] == row, 1.0, 0.0).astype(jnp.bfloat16)
    found = jnp.dot(hot, table_ref[...], preferred_element_type=jnp.float32)
    out_ref[...] = found.astype(jnp.bfloat16)


def lookup(me, ids, table, cap):
    groups, owners, _ = ids.shape
    rows, columns = table.shape
    count = groups * owners * cap
    chunk = 256
    return pl.pallas_call(
        functools.partial(lookup_kernel, cap),
        grid=(count // chunk,),
        in_specs=[
            SMEM,
            pl.BlockSpec(ids.shape, lambda m: (0, 0, 0)),
            pl.BlockSpec(table.shape, lambda m: (0, 0)),
        ],
        out_specs=[
            pl.BlockSpec((chunk, columns), lambda m: (m, 0)),
            pl.BlockSpec((chunk, LANES), lambda m: (m, 0)),
        ],
        out_shape=[
            jax.ShapeDtypeStruct((count, columns), jnp.bfloat16),
            jax.ShapeDtypeStruct((count, LANES), jnp.int32),
        ],
        scratch_shapes=[pltpu.VMEM((count, LANES), jnp.int32)],
        name="lookup",
    )(me, ids, table)


def cut_kernel(me_ref, slot_ref, cot_ref, *out_refs):
    groups = len(out_refs)
    tokens, width = cot_ref.shape
    columns = width // groups
    slot = jnp.broadcast_to(slot_ref[...].astype(jnp.float32), (EXTRA, tokens)).astype(jnp.bfloat16)
    for d, out_ref in enumerate(out_refs):
        at = pl.multiple_of(lax.rem(me_ref[0] + d, groups) * columns, columns)
        out_ref[:tokens, :] = cot_ref[:, pl.ds(at, columns)]
        out_ref[tokens:, :] = jnp.concatenate([slot] * (columns // tokens), axis=1)


def cut(me, slot, cotangent, groups):
    tokens, width = cotangent.shape
    piece = jax.ShapeDtypeStruct((tokens + EXTRA, width // groups), jnp.bfloat16)
    return pl.pallas_call(
        cut_kernel,
        in_specs=[SMEM, VMEM, VMEM],
        out_specs=[VMEM] * groups,
        out_shape=[piece] * groups,
        name="cut",
    )(me, slot, cotangent)


def target_line(slot, cap, part, parts):
    return lax.div(slot, cap) * (parts * cap) + part * cap + lax.rem(slot, cap)


def slots_of(piece_ref):
    tokens = piece_ref.shape[0] - EXTRA
    return piece_ref[tokens:, :tokens].astype(jnp.float32)[:1].astype(jnp.int32)


def pack_kernel(cap, *refs):
    piece_refs, out_ref = refs[:-1], refs[-1]
    groups = len(piece_refs)
    owners = out_ref.shape[0]
    tokens = piece_refs[0].shape[0] - EXTRA
    columns = out_ref.shape[2]
    parts = groups // 2
    line = lax.broadcasted_iota(jnp.int32, (owners * parts * cap, tokens), 0)
    for half in range(2):
        group = piece_refs[half * parts : (half + 1) * parts]
        hot = jnp.concatenate(
            [
                jnp.where(line == target_line(slots_of(ref), cap, part, parts), 1.0, 0.0).astype(jnp.bfloat16)
                for part, ref in enumerate(group)
            ],
            axis=1,
        )
        right = jnp.concatenate([ref[:tokens, :] for ref in group], axis=0)
        placed = jnp.dot(hot, right, preferred_element_type=jnp.float32).astype(jnp.bfloat16)
        out_ref[:, half * parts * cap : (half + 1) * parts * cap, :] = placed.reshape(owners, parts * cap, columns)


def pack(pieces, owners, cap):
    groups = len(pieces)
    return pl.pallas_call(
        functools.partial(pack_kernel, cap),
        in_specs=[VMEM] * groups,
        out_specs=VMEM,
        out_shape=jax.ShapeDtypeStruct((owners, groups * cap, pieces[0].shape[1]), jnp.bfloat16),
        name="pack",
    )(*pieces)


def unpack_kernel(cap, groups, *refs):
    piece_refs, got_ref, out_refs = refs[:groups], refs[groups], refs[groups + 1 :]
    owners, _, columns = got_ref.shape
    tokens = out_refs[0].shape[0]
    parts = groups // 2
    line = lax.broadcasted_iota(jnp.int32, (tokens, owners * parts * cap), 1)
    for half in range(2):
        group = piece_refs[half * parts : (half + 1) * parts]
        hot = jnp.concatenate(
            [
                jnp.where(
                    line == to_column(target_line(slots_of(ref), cap, part, parts)), 1.0, 0.0
                ).astype(jnp.bfloat16)
                for part, ref in enumerate(group)
            ],
            axis=0,
        )
        right = got_ref[:, half * parts * cap : (half + 1) * parts * cap, :].reshape(-1, columns)
        picked = jnp.dot(hot, right, preferred_element_type=jnp.float32).astype(jnp.bfloat16)
        for part in range(parts):
            out_refs[half * parts + part][...] = picked[part * tokens : (part + 1) * tokens]


def unpack(pieces, got, cap):
    groups = len(pieces)
    tokens = pieces[0].shape[0] - EXTRA
    return pl.pallas_call(
        functools.partial(unpack_kernel, cap, groups),
        in_specs=[VMEM] * (groups + 1),
        out_specs=[VMEM] * groups,
        out_shape=[jax.ShapeDtypeStruct((tokens, got.shape[2]), jnp.bfloat16)] * groups,
        name="unpack",
    )(*pieces, got)


def join_kernel(me_ref, *refs):
    out_ref = refs[-1]
    groups = len(refs) - 1
    for d, ref in enumerate(refs[:-1]):
        columns = ref.shape[1]
        at = pl.multiple_of(lax.rem(me_ref[0] + d, groups) * columns, columns)
        out_ref[:, pl.ds(at, columns)] = ref[...]


def join(me, pieces):
    tokens, columns = pieces[0].shape
    return pl.pallas_call(
        join_kernel,
        in_specs=[SMEM] + [VMEM] * len(pieces),
        out_specs=VMEM,
        out_shape=jax.ShapeDtypeStruct((tokens, columns * len(pieces)), jnp.bfloat16),
        name="join",
    )(me, *pieces)


def exchange(x, axes):
    return lax.all_to_all(x, axes, split_axis=0, concat_axis=0, tiled=True)


def pass_on(pieces, sign):
    size = len(pieces)
    moved = [lax.ppermute(pieces[d], "group", [(i, (i + sign * d) % size) for i in range(size)]) for d in range(1, size)]
    return [pieces[0], *moved]


def per_device(shard_ids, row_ids, table, cotangent):
    tokens, width = cotangent.shape
    groups = lax.axis_size("group")
    owners = lax.axis_size("vocab")
    cap = 2 * tokens // owners
    rows_here, columns = table.shape
    me = lax.axis_index("group").astype(jnp.int32).reshape(1)
    ids, slot = slots(shard_ids.reshape(1, tokens), row_ids.reshape(1, tokens), owners, cap)
    ids = exchange(ids.reshape(owners, 1, LANES), "vocab")
    ids = lax.all_gather(ids.reshape(owners, LANES), "group", axis=0)
    pieces = cut(me, slot, cotangent, groups)
    found, lines = lookup(me, ids, table, cap)
    found, pieces = lax.optimization_barrier((found, pieces))
    got = exchange(found.reshape(owners, groups * cap, columns), "vocab")
    pieces = pass_on(pieces, 1)
    arrived = exchange(pack(pieces, owners, cap), "vocab")
    embeds = join(me, pass_on(unpack(pieces, got, cap), -1))
    wanted = lines[:, 0] - 1
    picker = (jnp.arange(rows_here, dtype=jnp.int32)[:, None] == wanted[None, :]).astype(jnp.bfloat16)
    picker = lax.optimization_barrier(picker)
    table_grad = jnp.dot(picker, arrived.reshape(-1, columns), preferred_element_type=jnp.float32)
    return (embeds, table_grad.astype(jnp.bfloat16))


def solution(mesh):
    in_specs = (
        P(("group", "vocab"), None),
        P(("group", "vocab")),
        P("vocab", "group"),
        P(("group", "vocab"), None),
    )
    out_specs = (P(("group", "vocab"), None), P("vocab", "group"))
    return jax.shard_map(
        per_device, mesh=mesh, in_specs=in_specs, out_specs=out_specs, check_vma=False
    )
```

```python
import functools

import jax
import jax.numpy as jnp
from jax import lax
from jax.experimental import pallas as pl
from jax.experimental.pallas import tpu as pltpu
from jax.sharding import PartitionSpec as P

LANES = 128


def to_column(row):
    n = row.shape[1]
    here = lax.broadcasted_iota(jnp.int32, (n, n), 0)
    there = lax.broadcasted_iota(jnp.int32, (n, n), 1)
    return jnp.sum(jnp.where(here == there, row, 0), axis=1, keepdims=True)


def slots_kernel(cap, shard_ref, row_ref, ids_ref, slot_ref):
    tokens = shard_ref.shape[1]
    owners = ids_ref.shape[0]
    shard = shard_ref[...]
    i = lax.broadcasted_iota(jnp.int32, (tokens, tokens), 0)
    j = lax.broadcasted_iota(jnp.int32, (tokens, tokens), 1)
    earlier = jnp.where((to_column(shard) == shard) & (i < j), 1, 0)
    slot = shard * cap + jnp.sum(earlier, axis=0, keepdims=True)
    slot_ref[...] = slot
    first = cap * lax.broadcasted_iota(jnp.int32, (owners, tokens), 0)
    lane = lax.broadcasted_iota(jnp.int32, (owners, LANES), 1)
    name = row_ref[...] + 1
    ids = jnp.zeros((owners, LANES), jnp.int32)
    for w in range(cap // 2):
        named = jnp.where(slot == first + 2 * w, name, 0) + jnp.where(slot == first + 2 * w + 1, name << 16, 0)
        ids = jnp.where(lane == w, jnp.sum(named, axis=1, keepdims=True), ids)
    ids_ref[...] = ids


def slots(shard, row, owners, cap):
    return pl.pallas_call(
        functools.partial(slots_kernel, cap),
        out_shape=[
            jax.ShapeDtypeStruct((owners, LANES), jnp.int32),
            jax.ShapeDtypeStruct(shard.shape, jnp.int32),
        ],
        name="slots",
    )(shard, row)


def pack_kernel(pieces, owners, slot_ref, cot_ref, out_ref, hot):
    tokens = slot_ref.shape[1]
    rows = hot.shape[0]

    @pl.when(pl.program_id(0) == 0)
    def _():
        line = lax.broadcasted_iota(jnp.int32, (rows, tokens), 0)
        for c in range(pieces):
            hot[:, c * tokens : (c + 1) * tokens] = jnp.where(
                line == slot_ref[...] * pieces + c, 1.0, 0.0
            ).astype(jnp.bfloat16)

    groups = cot_ref.shape[1] // (pieces * LANES)
    right = []
    for g in range(groups):
        right.append(
            jnp.concatenate(
                [cot_ref[:, (g * pieces + c) * LANES : (g * pieces + c + 1) * LANES] for c in range(pieces)],
                axis=0,
            )
        )
    placed = jnp.dot(hot[...], jnp.concatenate(right, axis=1), preferred_element_type=jnp.float32)
    placed = placed.astype(jnp.bfloat16)
    for g in range(groups):
        block = placed[:, g * LANES : (g + 1) * LANES]
        out_ref[g * owners : (g + 1) * owners] = block.reshape(owners, rows // owners, LANES)


def pack(slot, cotangent, groups, owners, cap):
    tokens, width = cotangent.shape
    pieces = width // groups // LANES
    rows = owners * cap * pieces
    step = 2
    return pl.pallas_call(
        functools.partial(pack_kernel, pieces, owners),
        grid=(groups // step,),
        in_specs=[
            pl.BlockSpec((1, tokens), lambda g: (0, 0)),
            pl.BlockSpec((tokens, step * pieces * LANES), lambda g: (0, g)),
        ],
        out_specs=pl.BlockSpec((step * owners, cap * pieces, LANES), lambda g: (g, 0, 0)),
        out_shape=jax.ShapeDtypeStruct((groups * owners, cap * pieces, LANES), jnp.bfloat16),
        scratch_shapes=[pltpu.VMEM((rows, pieces * tokens), jnp.bfloat16)],
        cost_estimate=pl.CostEstimate(
            flops=2 * rows * pieces * tokens * groups * LANES,
            bytes_accessed=2 * (tokens * width + groups * rows * LANES),
            transcendentals=0,
        ),
        name="pack",
    )(slot, cotangent)


def pick_kernel(ids_ref, out_ref):
    ids = ids_ref[...]
    owners, lanes = ids.shape
    lane = lax.broadcasted_iota(jnp.int32, (owners, lanes), 1)
    line = lax.broadcasted_iota(jnp.int32, (owners, lanes), 0)
    out = jnp.zeros((owners, lanes), jnp.int32)
    for w in range(out_ref.shape[1] // owners):
        word = jnp.sum(jnp.where(lane == w, ids, 0), axis=1, keepdims=True)
        out = jnp.where(lane == w * owners + line, word, out)
    out_ref[...] = jnp.sum(out, axis=0, keepdims=True)


def pick(ids, cap):
    owners = ids.shape[0]
    return pl.pallas_call(
        pick_kernel,
        out_shape=jax.ShapeDtypeStruct((1, cap // 2 * owners), jnp.int32),
        name="pick",
    )(ids)


def lookup_kernel(cap, words_ref, table_ref, out_ref, lines):
    groups = words_ref.shape[0]
    devices = out_ref.shape[0]
    rows, columns = table_ref.shape
    owners = devices // groups
    pieces = columns // LANES
    here = lax.broadcasted_iota(jnp.int32, (owners, cap // 2 * owners), 0)
    there = lax.broadcasted_iota(jnp.int32, (owners, cap // 2 * owners), 1)
    row = lax.broadcasted_iota(jnp.int32, (devices, rows), 1) + 1
    for w in range(cap // 2):
        word = jnp.concatenate(
            [
                jnp.sum(jnp.where(there == here + w * owners, words_ref[g], 0), axis=1, keepdims=True)
                for g in range(groups)
            ],
            axis=0,
        )
        for half in range(2):
            name = word >> 16 if half else word & 0xFFFF
            hot = jnp.where(name == row, 1.0, 0.0).astype(jnp.bfloat16)
            found = jnp.dot(hot, table_ref[...], preferred_element_type=jnp.float32)
            for c in range(pieces):
                line = (2 * w + half) * pieces + c
                lines[pl.ds(line, devices, stride=cap * pieces), :] = found[:, c * LANES : (c + 1) * LANES]
    out_ref[...] = lines[...].astype(jnp.bfloat16).reshape(out_ref.shape)


def lookup(words, table, owners, cap):
    groups = words.shape[0]
    rows, columns = table.shape
    pieces = columns // LANES
    step = 2
    return pl.pallas_call(
        functools.partial(lookup_kernel, cap),
        grid=(groups // step,),
        in_specs=[
            pl.BlockSpec((step, 1, words.shape[2]), lambda g: (g, 0, 0)),
            pl.BlockSpec((rows, columns), lambda g: (0, 0)),
        ],
        out_specs=pl.BlockSpec((step * owners, cap * pieces, LANES), lambda g: (g, 0, 0)),
        out_shape=jax.ShapeDtypeStruct((groups * owners, cap * pieces, LANES), jnp.bfloat16),
        scratch_shapes=[pltpu.VMEM((step * owners * cap * pieces, LANES), jnp.float32)],
        cost_estimate=pl.CostEstimate(
            flops=2 * groups * owners * cap * rows * columns,
            bytes_accessed=2 * (rows * columns + groups * owners * cap * columns),
            transcendentals=0,
        ),
        name="lookup",
    )(words, table)


def unpack_kernel(pieces, slot_ref, got_ref, out_ref, hot, wide):
    tokens, places = hot.shape
    lines = wide.shape[0]

    @pl.when(pl.program_id(0) == 0)
    def _():
        line = lax.broadcasted_iota(jnp.int32, (tokens, places), 1)
        hot[...] = jnp.where(line == to_column(slot_ref[...]), 1.0, 0.0).astype(jnp.bfloat16)

    columns = pieces * LANES
    groups = out_ref.shape[1] // columns
    owners = got_ref.shape[0] // groups
    for g in range(groups):
        wide[...] = got_ref[g * owners : (g + 1) * owners].reshape(lines, LANES).astype(jnp.float32)
        rows = jnp.concatenate(
            [wide[pl.ds(c, places, stride=pieces), :].astype(jnp.bfloat16) for c in range(pieces)], axis=1
        )
        picked = jnp.dot(hot[...], rows, preferred_element_type=jnp.float32)
        out_ref[:, g * columns : (g + 1) * columns] = picked.astype(jnp.bfloat16)


def unpack(slot, got, groups, width):
    tokens = slot.shape[1]
    pieces = width // groups // LANES
    owners = got.shape[0] // groups
    lines = owners * got.shape[1]
    step = groups // 2
    return pl.pallas_call(
        functools.partial(unpack_kernel, pieces),
        grid=(groups // step,),
        in_specs=[
            pl.BlockSpec((1, tokens), lambda g: (0, 0)),
            pl.BlockSpec((step * owners, got.shape[1], LANES), lambda g: (g, 0, 0)),
        ],
        out_specs=pl.BlockSpec((tokens, step * pieces * LANES), lambda g: (0, g)),
        out_shape=jax.ShapeDtypeStruct((tokens, width), jnp.bfloat16),
        scratch_shapes=[
            pltpu.VMEM((tokens, lines // pieces), jnp.bfloat16),
            pltpu.VMEM((lines, LANES), jnp.float32),
        ],
        name="unpack",
    )(slot, got)


def exchange(x, axes):
    return lax.all_to_all(x, axes, split_axis=0, concat_axis=0, tiled=True)


def per_device(shard_ids, row_ids, table, cotangent):
    tokens, width = cotangent.shape
    groups = lax.axis_size("group")
    owners = lax.axis_size("vocab")
    cap = 2 * tokens // owners
    peers = groups * owners
    rows_here, columns = table.shape
    outgoing, slot = slots(shard_ids.reshape(1, tokens), row_ids.reshape(1, tokens), owners, cap)
    ids = exchange(outgoing.reshape(owners, 1, LANES), "vocab")
    packed = pack(slot, cotangent, groups, owners, cap)
    ids, packed = lax.optimization_barrier((ids, packed))
    arrived = exchange(packed, ("group", "vocab"))
    words = lax.all_gather(pick(ids.reshape(owners, LANES), cap), "group", axis=0)
    got = exchange(lookup(words, table, owners, cap), ("group", "vocab"))
    words = words.reshape(groups, cap // 2, owners)
    wanted = jnp.stack([words & 0xFFFF, words >> 16], axis=2).reshape(groups, cap, owners)
    wanted = jnp.swapaxes(wanted, 1, 2).reshape(-1) - 1
    picker = (wanted[:, None] == jnp.arange(rows_here, dtype=jnp.int32)[None, :]).astype(jnp.bfloat16)
    table_grad = lax.dot_general(
        picker,
        arrived.reshape(peers * cap, columns),
        (((0,), (0,)), ((), ())),
        preferred_element_type=jnp.float32,
    )
    embeds = unpack(slot, got, groups, width)
    return (embeds, table_grad.astype(jnp.bfloat16))


def solution(mesh):
    in_specs = (
        P(("group", "vocab"), None),
        P(("group", "vocab")),
        P("vocab", "group"),
        P(("group", "vocab"), None),
    )
    out_specs = (P(("group", "vocab"), None), P("vocab", "group"))
    return jax.shard_map(
        per_device, mesh=mesh, in_specs=in_specs, out_specs=out_specs, check_vma=False
    )
```

```python
import functools

import jax
import jax.numpy as jnp
from jax import lax
from jax.experimental import pallas as pl
from jax.experimental.pallas import tpu as pltpu
from jax.sharding import PartitionSpec as P

LANES = 128


def to_column(row):
    n = row.shape[1]
    here = lax.broadcasted_iota(jnp.int32, (n, n), 0)
    there = lax.broadcasted_iota(jnp.int32, (n, n), 1)
    return jnp.sum(jnp.where(here == there, row, 0), axis=1, keepdims=True)


def slots_kernel(cap, shard_ref, row_ref, ids_ref, slot_ref):
    tokens = shard_ref.shape[1]
    owners = ids_ref.shape[0]
    shard = shard_ref[...]
    i = lax.broadcasted_iota(jnp.int32, (tokens, tokens), 0)
    j = lax.broadcasted_iota(jnp.int32, (tokens, tokens), 1)
    earlier = jnp.where((to_column(shard) == shard) & (i < j), 1, 0)
    slot = shard * cap + jnp.sum(earlier, axis=0, keepdims=True)
    slot_ref[...] = slot
    first = cap * lax.broadcasted_iota(jnp.int32, (owners, tokens), 0)
    lane = lax.broadcasted_iota(jnp.int32, (owners, LANES), 1)
    name = row_ref[...] + 1
    ids = jnp.zeros((owners, LANES), jnp.int32)
    for w in range(cap // 2):
        named = jnp.where(slot == first + 2 * w, name, 0) + jnp.where(slot == first + 2 * w + 1, name << 16, 0)
        ids = jnp.where(lane == w, jnp.sum(named, axis=1, keepdims=True), ids)
    ids_ref[...] = ids


def slots(shard, row, owners, cap):
    return pl.pallas_call(
        functools.partial(slots_kernel, cap),
        out_shape=[
            jax.ShapeDtypeStruct((owners, LANES), jnp.int32),
            jax.ShapeDtypeStruct(shard.shape, jnp.int32),
        ],
        name="slots",
    )(shard, row)


def pack_kernel(pieces, owners, slot_ref, cot_ref, out_ref, hot, wide):
    places, tokens = hot.shape
    lines = wide.shape[1]

    @pl.when(pl.program_id(0) == 0)
    def _():
        line = lax.broadcasted_iota(jnp.int32, (places, tokens), 0)
        hot[...] = jnp.where(line == slot_ref[...], 1.0, 0.0).astype(jnp.bfloat16)

    columns = pieces * LANES
    for g in range(cot_ref.shape[1] // columns):
        placed = jnp.dot(
            hot[...], cot_ref[:, g * columns : (g + 1) * columns], preferred_element_type=jnp.float32
        )
        for c in range(pieces):
            wide[g % 2, pl.ds(c, places, stride=pieces), :] = placed[:, c * LANES : (c + 1) * LANES]
        block = wide[g % 2].astype(jnp.bfloat16)
        out_ref[g * owners : (g + 1) * owners] = block.reshape(owners, lines // owners, LANES)


def pack(slot, cotangent, groups, owners, cap):
    tokens, width = cotangent.shape
    pieces = width // groups // LANES
    places = owners * cap
    lines = places * pieces
    step = groups // 2
    return pl.pallas_call(
        functools.partial(pack_kernel, pieces, owners),
        grid=(groups // step,),
        in_specs=[
            pl.BlockSpec((1, tokens), lambda g: (0, 0)),
            pl.BlockSpec((tokens, step * pieces * LANES), lambda g: (0, g)),
        ],
        out_specs=pl.BlockSpec((step * owners, cap * pieces, LANES), lambda g: (g, 0, 0)),
        out_shape=jax.ShapeDtypeStruct((groups * owners, cap * pieces, LANES), jnp.bfloat16),
        scratch_shapes=[
            pltpu.VMEM((places, tokens), jnp.bfloat16),
            pltpu.VMEM((2, lines, LANES), jnp.float32),
        ],
        cost_estimate=pl.CostEstimate(
            flops=2 * places * tokens * width,
            bytes_accessed=2 * (tokens * width + groups * lines * LANES),
            transcendentals=0,
        ),
        name="pack",
    )(slot, cotangent)


def pick_kernel(ids_ref, out_ref):
    ids = ids_ref[...]
    owners, lanes = ids.shape
    lane = lax.broadcasted_iota(jnp.int32, (owners, lanes), 1)
    line = lax.broadcasted_iota(jnp.int32, (owners, lanes), 0)
    out = jnp.zeros((owners, lanes), jnp.int32)
    for w in range(out_ref.shape[1] // owners):
        word = jnp.sum(jnp.where(lane == w, ids, 0), axis=1, keepdims=True)
        out = jnp.where(lane == w * owners + line, word, out)
    out_ref[...] = jnp.sum(out, axis=0, keepdims=True)


def pick(ids, cap):
    owners = ids.shape[0]
    return pl.pallas_call(
        pick_kernel,
        out_shape=jax.ShapeDtypeStruct((1, cap // 2 * owners), jnp.int32),
        name="pick",
    )(ids)


def lookup_kernel(cap, words_ref, table_ref, out_ref, lines):
    groups = words_ref.shape[0]
    devices = out_ref.shape[0]
    rows, columns = table_ref.shape
    owners = devices // groups
    pieces = columns // LANES
    here = lax.broadcasted_iota(jnp.int32, (owners, cap // 2 * owners), 0)
    there = lax.broadcasted_iota(jnp.int32, (owners, cap // 2 * owners), 1)
    row = lax.broadcasted_iota(jnp.int32, (devices, rows), 1) + 1
    for w in range(cap // 2):
        word = jnp.concatenate(
            [
                jnp.sum(jnp.where(there == here + w * owners, words_ref[g], 0), axis=1, keepdims=True)
                for g in range(groups)
            ],
            axis=0,
        )
        for half in range(2):
            name = word >> 16 if half else word & 0xFFFF
            hot = jnp.where(name == row, 1.0, 0.0).astype(jnp.bfloat16)
            found = jnp.dot(hot, table_ref[...], preferred_element_type=jnp.float32)
            for c in range(pieces):
                line = (2 * w + half) * pieces + c
                lines[pl.ds(line, devices, stride=cap * pieces), :] = found[:, c * LANES : (c + 1) * LANES]
    out_ref[...] = lines[...].astype(jnp.bfloat16).reshape(out_ref.shape)


def lookup(words, table, owners, cap):
    groups = words.shape[0]
    rows, columns = table.shape
    pieces = columns // LANES
    step = 2
    return pl.pallas_call(
        functools.partial(lookup_kernel, cap),
        grid=(groups // step,),
        in_specs=[
            pl.BlockSpec((step, 1, words.shape[2]), lambda g: (g, 0, 0)),
            pl.BlockSpec((rows, columns), lambda g: (0, 0)),
        ],
        out_specs=pl.BlockSpec((step * owners, cap * pieces, LANES), lambda g: (g, 0, 0)),
        out_shape=jax.ShapeDtypeStruct((groups * owners, cap * pieces, LANES), jnp.bfloat16),
        scratch_shapes=[pltpu.VMEM((step * owners * cap * pieces, LANES), jnp.float32)],
        cost_estimate=pl.CostEstimate(
            flops=2 * groups * owners * cap * rows * columns,
            bytes_accessed=2 * (rows * columns + groups * owners * cap * columns),
            transcendentals=0,
        ),
        name="lookup",
    )(words, table)


def unpack_kernel(pieces, slot_ref, got_ref, out_ref, hot, wide):
    tokens, places = hot.shape
    lines = wide.shape[0]

    @pl.when(pl.program_id(0) == 0)
    def _():
        line = lax.broadcasted_iota(jnp.int32, (tokens, places), 1)
        hot[...] = jnp.where(line == to_column(slot_ref[...]), 1.0, 0.0).astype(jnp.bfloat16)

    columns = pieces * LANES
    groups = out_ref.shape[1] // columns
    owners = got_ref.shape[0] // groups
    for g in range(groups):
        wide[...] = got_ref[g * owners : (g + 1) * owners].reshape(lines, LANES).astype(jnp.float32)
        rows = jnp.concatenate(
            [wide[pl.ds(c, places, stride=pieces), :].astype(jnp.bfloat16) for c in range(pieces)], axis=1
        )
        picked = jnp.dot(hot[...], rows, preferred_element_type=jnp.float32)
        out_ref[:, g * columns : (g + 1) * columns] = picked.astype(jnp.bfloat16)


def unpack(slot, got, groups, width):
    tokens = slot.shape[1]
    pieces = width // groups // LANES
    owners = got.shape[0] // groups
    lines = owners * got.shape[1]
    step = groups // 2
    return pl.pallas_call(
        functools.partial(unpack_kernel, pieces),
        grid=(groups // step,),
        in_specs=[
            pl.BlockSpec((1, tokens), lambda g: (0, 0)),
            pl.BlockSpec((step * owners, got.shape[1], LANES), lambda g: (g, 0, 0)),
        ],
        out_specs=pl.BlockSpec((tokens, step * pieces * LANES), lambda g: (0, g)),
        out_shape=jax.ShapeDtypeStruct((tokens, width), jnp.bfloat16),
        scratch_shapes=[
            pltpu.VMEM((tokens, lines // pieces), jnp.bfloat16),
            pltpu.VMEM((lines, LANES), jnp.float32),
        ],
        name="unpack",
    )(slot, got)


def exchange(x, axes):
    return lax.all_to_all(x, axes, split_axis=0, concat_axis=0, tiled=True)


def per_device(shard_ids, row_ids, table, cotangent):
    tokens, width = cotangent.shape
    groups = lax.axis_size("group")
    owners = lax.axis_size("vocab")
    cap = 2 * tokens // owners
    peers = groups * owners
    rows_here, columns = table.shape
    outgoing, slot = slots(shard_ids.reshape(1, tokens), row_ids.reshape(1, tokens), owners, cap)
    ids = exchange(outgoing.reshape(owners, 1, LANES), "vocab")
    packed = pack(slot, cotangent, groups, owners, cap)
    ids, packed = lax.optimization_barrier((ids, packed))
    arrived = exchange(packed, ("group", "vocab"))
    words = lax.all_gather(pick(ids.reshape(owners, LANES), cap), "group", axis=0)
    got = exchange(lookup(words, table, owners, cap), ("group", "vocab"))
    words = words.reshape(groups, cap // 2, owners)
    wanted = jnp.stack([words & 0xFFFF, words >> 16], axis=2).reshape(groups, cap, owners)
    wanted = jnp.swapaxes(wanted, 1, 2).reshape(-1) - 1
    picker = (wanted[:, None] == jnp.arange(rows_here, dtype=jnp.int32)[None, :]).astype(jnp.bfloat16)
    table_grad = lax.dot_general(
        picker,
        arrived.reshape(peers * cap, columns),
        (((0,), (0,)), ((), ())),
        preferred_element_type=jnp.float32,
    )
    embeds = unpack(slot, got, groups, width)
    return (embeds, table_grad.astype(jnp.bfloat16))


def solution(mesh):
    in_specs = (
        P(("group", "vocab"), None),
        P(("group", "vocab")),
        P("vocab", "group"),
        P(("group", "vocab"), None),
    )
    out_specs = (P(("group", "vocab"), None), P("vocab", "group"))
    return jax.shard_map(
        per_device, mesh=mesh, in_specs=in_specs, out_specs=out_specs, check_vma=False
    )
```

```python
import functools

import jax
import jax.numpy as jnp
from jax import lax
from jax.experimental import pallas as pl
from jax.experimental.pallas import tpu as pltpu
from jax.sharding import PartitionSpec as P

LANES = 128


def to_column(row):
    n = row.shape[1]
    here = lax.broadcasted_iota(jnp.int32, (n, n), 0)
    there = lax.broadcasted_iota(jnp.int32, (n, n), 1)
    return jnp.sum(jnp.where(here == there, row, 0), axis=1, keepdims=True)


def slots_kernel(cap, shard_ref, row_ref, ids_ref, slot_ref):
    tokens = shard_ref.shape[1]
    owners = ids_ref.shape[0]
    shard = shard_ref[...]
    i = lax.broadcasted_iota(jnp.int32, (tokens, tokens), 0)
    j = lax.broadcasted_iota(jnp.int32, (tokens, tokens), 1)
    earlier = jnp.where((to_column(shard) == shard) & (i < j), 1, 0)
    slot = shard * cap + jnp.sum(earlier, axis=0, keepdims=True)
    slot_ref[...] = slot
    first = cap * lax.broadcasted_iota(jnp.int32, (owners, tokens), 0)
    lane = lax.broadcasted_iota(jnp.int32, (owners, LANES), 1)
    name = row_ref[...] + 1
    ids = jnp.zeros((owners, LANES), jnp.int32)
    for w in range(cap // 2):
        named = jnp.where(slot == first + 2 * w, name, 0) + jnp.where(slot == first + 2 * w + 1, name << 16, 0)
        ids = jnp.where(lane == w, jnp.sum(named, axis=1, keepdims=True), ids)
    ids_ref[...] = ids


def slots(shard, row, owners, cap):
    return pl.pallas_call(
        functools.partial(slots_kernel, cap),
        out_shape=[
            jax.ShapeDtypeStruct((owners, LANES), jnp.int32),
            jax.ShapeDtypeStruct(shard.shape, jnp.int32),
        ],
        name="slots",
    )(shard, row)


def pack_kernel(pieces, owners, slot_ref, cot_ref, out_ref, hot, wide):
    places, tokens = hot.shape
    lines = wide.shape[1]

    @pl.when(pl.program_id(0) == 0)
    def _():
        line = lax.broadcasted_iota(jnp.int32, (places, tokens), 0)
        hot[...] = jnp.where(line == slot_ref[...], 1.0, 0.0).astype(jnp.bfloat16)

    columns = pieces * LANES
    for g in range(cot_ref.shape[1] // columns):
        placed = jnp.dot(
            hot[...], cot_ref[:, g * columns : (g + 1) * columns], preferred_element_type=jnp.float32
        )
        for c in range(pieces):
            wide[g % 2, pl.ds(c, places, stride=pieces), :] = placed[:, c * LANES : (c + 1) * LANES]
        block = wide[g % 2].astype(jnp.bfloat16)
        out_ref[g * owners : (g + 1) * owners] = block.reshape(owners, lines // owners, LANES)


def pack(slot, cotangent, groups, owners, cap):
    tokens, width = cotangent.shape
    pieces = width // groups // LANES
    places = owners * cap
    lines = places * pieces
    step = groups // 2
    return pl.pallas_call(
        functools.partial(pack_kernel, pieces, owners),
        grid=(groups // step,),
        in_specs=[
            pl.BlockSpec((1, tokens), lambda g: (0, 0)),
            pl.BlockSpec((tokens, step * pieces * LANES), lambda g: (0, g)),
        ],
        out_specs=pl.BlockSpec((step * owners, cap * pieces, LANES), lambda g: (g, 0, 0)),
        out_shape=jax.ShapeDtypeStruct((groups * owners, cap * pieces, LANES), jnp.bfloat16),
        scratch_shapes=[
            pltpu.VMEM((places, tokens), jnp.bfloat16),
            pltpu.VMEM((2, lines, LANES), jnp.float32),
        ],
        cost_estimate=pl.CostEstimate(
            flops=2 * places * tokens * width,
            bytes_accessed=2 * (tokens * width + groups * lines * LANES),
            transcendentals=0,
        ),
        name="pack",
    )(slot, cotangent)


def lookup_kernel(cap, words_ref, table_ref, out_ref, lines):
    groups = words_ref.shape[0]
    devices = out_ref.shape[0]
    rows, columns = table_ref.shape
    owners = devices // groups
    pieces = columns // LANES
    here = lax.broadcasted_iota(jnp.int32, (owners, cap // 2 * owners), 0)
    there = lax.broadcasted_iota(jnp.int32, (owners, cap // 2 * owners), 1)
    row = lax.broadcasted_iota(jnp.int32, (devices, rows), 1) + 1
    for w in range(cap // 2):
        word = jnp.concatenate(
            [
                jnp.sum(jnp.where(there == here + w * owners, words_ref[g], 0), axis=1, keepdims=True)
                for g in range(groups)
            ],
            axis=0,
        )
        for half in range(2):
            name = word >> 16 if half else word & 0xFFFF
            hot = jnp.where(name == row, 1.0, 0.0).astype(jnp.bfloat16)
            found = jnp.dot(hot, table_ref[...], preferred_element_type=jnp.float32)
            for c in range(pieces):
                line = (2 * w + half) * pieces + c
                lines[pl.ds(line, devices, stride=cap * pieces), :] = found[:, c * LANES : (c + 1) * LANES]
    out_ref[...] = lines[...].astype(jnp.bfloat16).reshape(out_ref.shape)


def lookup(words, table, owners, cap):
    groups = words.shape[0]
    rows, columns = table.shape
    pieces = columns // LANES
    step = 2
    return pl.pallas_call(
        functools.partial(lookup_kernel, cap),
        grid=(groups // step,),
        in_specs=[
            pl.BlockSpec((step, 1, words.shape[2]), lambda g: (g, 0, 0)),
            pl.BlockSpec((rows, columns), lambda g: (0, 0)),
        ],
        out_specs=pl.BlockSpec((step * owners, cap * pieces, LANES), lambda g: (g, 0, 0)),
        out_shape=jax.ShapeDtypeStruct((groups * owners, cap * pieces, LANES), jnp.bfloat16),
        scratch_shapes=[pltpu.VMEM((step * owners * cap * pieces, LANES), jnp.float32)],
        cost_estimate=pl.CostEstimate(
            flops=2 * groups * owners * cap * rows * columns,
            bytes_accessed=2 * (rows * columns + groups * owners * cap * columns),
            transcendentals=0,
        ),
        name="lookup",
    )(words, table)


def unpack_kernel(pieces, slot_ref, got_ref, out_ref, hot, wide):
    tokens, places = hot.shape
    lines = wide.shape[0]

    @pl.when(pl.program_id(0) == 0)
    def _():
        line = lax.broadcasted_iota(jnp.int32, (tokens, places), 1)
        hot[...] = jnp.where(line == to_column(slot_ref[...]), 1.0, 0.0).astype(jnp.bfloat16)

    columns = pieces * LANES
    groups = out_ref.shape[1] // columns
    owners = got_ref.shape[0] // groups
    for g in range(groups):
        wide[...] = got_ref[g * owners : (g + 1) * owners].reshape(lines, LANES).astype(jnp.float32)
        rows = jnp.concatenate(
            [wide[pl.ds(c, places, stride=pieces), :].astype(jnp.bfloat16) for c in range(pieces)], axis=1
        )
        picked = jnp.dot(hot[...], rows, preferred_element_type=jnp.float32)
        out_ref[:, g * columns : (g + 1) * columns] = picked.astype(jnp.bfloat16)


def unpack(slot, got, groups, width):
    tokens = slot.shape[1]
    pieces = width // groups // LANES
    owners = got.shape[0] // groups
    lines = owners * got.shape[1]
    step = groups // 2
    return pl.pallas_call(
        functools.partial(unpack_kernel, pieces),
        grid=(groups // step,),
        in_specs=[
            pl.BlockSpec((1, tokens), lambda g: (0, 0)),
            pl.BlockSpec((step * owners, got.shape[1], LANES), lambda g: (g, 0, 0)),
        ],
        out_specs=pl.BlockSpec((tokens, step * pieces * LANES), lambda g: (0, g)),
        out_shape=jax.ShapeDtypeStruct((tokens, width), jnp.bfloat16),
        scratch_shapes=[
            pltpu.VMEM((tokens, lines // pieces), jnp.bfloat16),
            pltpu.VMEM((lines, LANES), jnp.float32),
        ],
        name="unpack",
    )(slot, got)


def exchange(x, axes):
    return lax.all_to_all(x, axes, split_axis=0, concat_axis=0, tiled=True)


def per_device(shard_ids, row_ids, table, cotangent):
    tokens, width = cotangent.shape
    groups = lax.axis_size("group")
    owners = lax.axis_size("vocab")
    cap = 2 * tokens // owners
    peers = groups * owners
    rows_here, columns = table.shape
    outgoing, slot = slots(shard_ids.reshape(1, tokens), row_ids.reshape(1, tokens), owners, cap)
    ids = exchange(outgoing.reshape(owners, 1, LANES), "vocab")
    packed = pack(slot, cotangent, groups, owners, cap)
    ids, packed = lax.optimization_barrier((ids, packed))
    arrived = exchange(packed, ("group", "vocab"))
    mine = jnp.swapaxes(ids[:, 0, : cap // 2], 0, 1).reshape(1, cap // 2 * owners)
    words = lax.all_gather(mine, "group", axis=0)
    got = exchange(lookup(words, table, owners, cap), ("group", "vocab"))
    words = words.reshape(groups, cap // 2, owners)
    wanted = jnp.stack([words & 0xFFFF, words >> 16], axis=2).reshape(groups, cap, owners)
    wanted = jnp.swapaxes(wanted, 1, 2).reshape(-1) - 1
    picker = (wanted[:, None] == jnp.arange(rows_here, dtype=jnp.int32)[None, :]).astype(jnp.bfloat16)
    table_grad = lax.dot_general(
        picker,
        arrived.reshape(peers * cap, columns),
        (((0,), (0,)), ((), ())),
        preferred_element_type=jnp.float32,
    )
    embeds = unpack(slot, got, groups, width)
    return (embeds, table_grad.astype(jnp.bfloat16))


def solution(mesh):
    in_specs = (
        P(("group", "vocab"), None),
        P(("group", "vocab")),
        P("vocab", "group"),
        P(("group", "vocab"), None),
    )
    out_specs = (P(("group", "vocab"), None), P("vocab", "group"))
    return jax.shard_map(
        per_device, mesh=mesh, in_specs=in_specs, out_specs=out_specs, check_vma=False
    )
```

```python
import functools

import jax
import jax.numpy as jnp
from jax import lax
from jax.experimental import pallas as pl
from jax.experimental.pallas import tpu as pltpu
from jax.sharding import PartitionSpec as P

LANES = 128


def to_column(row):
    n = row.shape[1]
    here = lax.broadcasted_iota(jnp.int32, (n, n), 0)
    there = lax.broadcasted_iota(jnp.int32, (n, n), 1)
    return jnp.sum(jnp.where(here == there, row, 0), axis=1, keepdims=True)


def slots_kernel(cap, shard_ref, row_ref, ids_ref, slot_ref):
    tokens = shard_ref.shape[1]
    owners = ids_ref.shape[0]
    shard = shard_ref[...]
    i = lax.broadcasted_iota(jnp.int32, (tokens, tokens), 0)
    j = lax.broadcasted_iota(jnp.int32, (tokens, tokens), 1)
    earlier = jnp.where((to_column(shard) == shard) & (i < j), 1, 0)
    slot = shard * cap + jnp.sum(earlier, axis=0, keepdims=True)
    slot_ref[...] = slot
    first = cap * lax.broadcasted_iota(jnp.int32, (owners, tokens), 0)
    lane = lax.broadcasted_iota(jnp.int32, (owners, LANES), 1)
    name = row_ref[...] + 1
    ids = jnp.zeros((owners, LANES), jnp.int32)
    for w in range(cap // 2):
        named = jnp.where(slot == first + 2 * w, name, 0) + jnp.where(slot == first + 2 * w + 1, name << 16, 0)
        ids = jnp.where(lane == w, jnp.sum(named, axis=1, keepdims=True), ids)
    ids_ref[...] = ids


def slots(shard, row, owners, cap):
    return pl.pallas_call(
        functools.partial(slots_kernel, cap),
        out_shape=[
            jax.ShapeDtypeStruct((owners, LANES), jnp.int32),
            jax.ShapeDtypeStruct(shard.shape, jnp.int32),
        ],
        name="slots",
    )(shard, row)


def pack_kernel(pieces, owners, slot_ref, cot_ref, out_ref, hot, wide):
    places, tokens = hot.shape
    lines = wide.shape[1]

    @pl.when(pl.program_id(0) == 0)
    def _():
        line = lax.broadcasted_iota(jnp.int32, (places, tokens), 0)
        hot[...] = jnp.where(line == slot_ref[...], 1.0, 0.0).astype(jnp.bfloat16)

    columns = pieces * LANES
    for g in range(cot_ref.shape[1] // columns):
        placed = jnp.dot(
            hot[...], cot_ref[:, g * columns : (g + 1) * columns], preferred_element_type=jnp.float32
        )
        for c in range(pieces):
            wide[g % 2, pl.ds(c, places, stride=pieces), :] = placed[:, c * LANES : (c + 1) * LANES]
        block = wide[g % 2].astype(jnp.bfloat16)
        out_ref[g * owners : (g + 1) * owners] = block.reshape(owners, lines // owners, LANES)


def pack(slot, cotangent, groups, owners, cap):
    tokens, width = cotangent.shape
    pieces = width // groups // LANES
    places = owners * cap
    lines = places * pieces
    step = groups // 2
    return pl.pallas_call(
        functools.partial(pack_kernel, pieces, owners),
        grid=(groups // step,),
        in_specs=[
            pl.BlockSpec((1, tokens), lambda g: (0, 0)),
            pl.BlockSpec((tokens, step * pieces * LANES), lambda g: (0, g)),
        ],
        out_specs=pl.BlockSpec((step * owners, cap * pieces, LANES), lambda g: (g, 0, 0)),
        out_shape=jax.ShapeDtypeStruct((groups * owners, cap * pieces, LANES), jnp.bfloat16),
        scratch_shapes=[
            pltpu.VMEM((places, tokens), jnp.bfloat16),
            pltpu.VMEM((2, lines, LANES), jnp.float32),
        ],
        cost_estimate=pl.CostEstimate(
            flops=2 * places * tokens * width,
            bytes_accessed=2 * (tokens * width + groups * lines * LANES),
            transcendentals=0,
        ),
        name="pack",
    )(slot, cotangent)


def lookup_kernel(cap, slot_ref, words_ref, table_ref, out_ref, hot_ref, lines):
    @pl.when(pl.program_id(0) == 0)
    def _():
        place = lax.broadcasted_iota(jnp.int32, hot_ref.shape, 1)
        hot_ref[...] = jnp.where(place == to_column(slot_ref[...]), 1.0, 0.0).astype(jnp.bfloat16)

    groups = words_ref.shape[0]
    devices = out_ref.shape[0]
    rows, columns = table_ref.shape
    owners = devices // groups
    pieces = columns // LANES
    here = lax.broadcasted_iota(jnp.int32, (owners, cap // 2 * owners), 0)
    there = lax.broadcasted_iota(jnp.int32, (owners, cap // 2 * owners), 1)
    row = lax.broadcasted_iota(jnp.int32, (devices, rows), 1) + 1
    for w in range(cap // 2):
        word = jnp.concatenate(
            [
                jnp.sum(jnp.where(there == here + w * owners, words_ref[g], 0), axis=1, keepdims=True)
                for g in range(groups)
            ],
            axis=0,
        )
        for half in range(2):
            name = word >> 16 if half else word & 0xFFFF
            hot = jnp.where(name == row, 1.0, 0.0).astype(jnp.bfloat16)
            found = jnp.dot(hot, table_ref[...], preferred_element_type=jnp.float32)
            for c in range(pieces):
                line = (2 * w + half) * pieces + c
                lines[pl.ds(line, devices, stride=cap * pieces), :] = found[:, c * LANES : (c + 1) * LANES]
    out_ref[...] = lines[...].astype(jnp.bfloat16).reshape(out_ref.shape)


def lookup(slot, words, table, owners, cap):
    tokens = slot.shape[1]
    groups = words.shape[0]
    rows, columns = table.shape
    pieces = columns // LANES
    step = 2
    return pl.pallas_call(
        functools.partial(lookup_kernel, cap),
        grid=(groups // step,),
        in_specs=[
            pl.BlockSpec((1, tokens), lambda g: (0, 0)),
            pl.BlockSpec((step, 1, words.shape[2]), lambda g: (g, 0, 0)),
            pl.BlockSpec((rows, columns), lambda g: (0, 0)),
        ],
        out_specs=[
            pl.BlockSpec((step * owners, cap * pieces, LANES), lambda g: (g, 0, 0)),
            pl.BlockSpec((tokens, owners * cap), lambda g: (0, 0)),
        ],
        out_shape=[
            jax.ShapeDtypeStruct((groups * owners, cap * pieces, LANES), jnp.bfloat16),
            jax.ShapeDtypeStruct((tokens, owners * cap), jnp.bfloat16),
        ],
        scratch_shapes=[pltpu.VMEM((step * owners * cap * pieces, LANES), jnp.float32)],
        cost_estimate=pl.CostEstimate(
            flops=2 * groups * owners * cap * rows * columns,
            bytes_accessed=2 * (rows * columns + groups * owners * cap * columns),
            transcendentals=0,
        ),
        name="lookup",
    )(slot, words, table)


def unpack_kernel(pieces, hot_ref, got_ref, out_ref, wide):
    places = hot_ref.shape[1]
    lines = wide.shape[0]
    columns = pieces * LANES
    groups = out_ref.shape[1] // columns
    owners = got_ref.shape[0] // groups
    for g in range(groups):
        wide[...] = got_ref[g * owners : (g + 1) * owners].reshape(lines, LANES).astype(jnp.float32)
        rows = jnp.concatenate(
            [wide[pl.ds(c, places, stride=pieces), :].astype(jnp.bfloat16) for c in range(pieces)], axis=1
        )
        picked = jnp.dot(hot_ref[...], rows, preferred_element_type=jnp.float32)
        out_ref[:, g * columns : (g + 1) * columns] = picked.astype(jnp.bfloat16)


def unpack(hot, got, groups, width):
    tokens = hot.shape[0]
    pieces = width // groups // LANES
    owners = got.shape[0] // groups
    lines = owners * got.shape[1]
    step = groups // 2
    return pl.pallas_call(
        functools.partial(unpack_kernel, pieces),
        grid=(groups // step,),
        in_specs=[
            pl.BlockSpec(hot.shape, lambda g: (0, 0)),
            pl.BlockSpec((step * owners, got.shape[1], LANES), lambda g: (g, 0, 0)),
        ],
        out_specs=pl.BlockSpec((tokens, step * pieces * LANES), lambda g: (0, g)),
        out_shape=jax.ShapeDtypeStruct((tokens, width), jnp.bfloat16),
        scratch_shapes=[pltpu.VMEM((lines, LANES), jnp.float32)],
        name="unpack",
    )(hot, got)


def exchange(x, axes):
    return lax.all_to_all(x, axes, split_axis=0, concat_axis=0, tiled=True)


def per_device(shard_ids, row_ids, table, cotangent):
    tokens, width = cotangent.shape
    groups = lax.axis_size("group")
    owners = lax.axis_size("vocab")
    cap = 2 * tokens // owners
    peers = groups * owners
    rows_here, columns = table.shape
    outgoing, slot = slots(shard_ids.reshape(1, tokens), row_ids.reshape(1, tokens), owners, cap)
    ids = exchange(outgoing.reshape(owners, 1, LANES), "vocab")
    packed = pack(slot, cotangent, groups, owners, cap)
    ids, packed = lax.optimization_barrier((ids, packed))
    arrived = exchange(packed, ("group", "vocab"))
    mine = jnp.swapaxes(ids[:, 0, : cap // 2], 0, 1).reshape(1, cap // 2 * owners)
    words = lax.all_gather(mine, "group", axis=0)
    found, hot = lookup(slot, words, table, owners, cap)
    got = exchange(found, ("group", "vocab"))
    words = words.reshape(groups, cap // 2, owners)
    wanted = jnp.stack([words & 0xFFFF, words >> 16], axis=2).reshape(groups, cap, owners)
    wanted = jnp.swapaxes(wanted, 1, 2).reshape(-1) - 1
    picker = (wanted[:, None] == jnp.arange(rows_here, dtype=jnp.int32)[None, :]).astype(jnp.bfloat16)
    table_grad = lax.dot_general(
        picker,
        arrived.reshape(peers * cap, columns),
        (((0,), (0,)), ((), ())),
        preferred_element_type=jnp.float32,
    )
    embeds = unpack(hot, got, groups, width)
    return (embeds, table_grad.astype(jnp.bfloat16))


def solution(mesh):
    in_specs = (
        P(("group", "vocab"), None),
        P(("group", "vocab")),
        P("vocab", "group"),
        P(("group", "vocab"), None),
    )
    out_specs = (P(("group", "vocab"), None), P("vocab", "group"))
    return jax.shard_map(
        per_device, mesh=mesh, in_specs=in_specs, out_specs=out_specs, check_vma=False
    )
```

```python
import functools

import jax
import jax.numpy as jnp
from jax import lax
from jax.experimental import pallas as pl
from jax.experimental.pallas import tpu as pltpu
from jax.sharding import PartitionSpec as P

LANES = 128


def to_column(row):
    n = row.shape[1]
    here = lax.broadcasted_iota(jnp.int32, (n, n), 0)
    there = lax.broadcasted_iota(jnp.int32, (n, n), 1)
    return jnp.sum(jnp.where(here == there, row, 0), axis=1, keepdims=True)


def slots_kernel(cap, shard_ref, row_ref, ids_ref, slot_ref):
    tokens = shard_ref.shape[1]
    owners = ids_ref.shape[0]
    shard = shard_ref[...]
    i = lax.broadcasted_iota(jnp.int32, (tokens, tokens), 0)
    j = lax.broadcasted_iota(jnp.int32, (tokens, tokens), 1)
    earlier = jnp.where((to_column(shard) == shard) & (i < j), 1, 0)
    slot = shard * cap + jnp.sum(earlier, axis=0, keepdims=True)
    slot_ref[...] = slot
    first = cap * lax.broadcasted_iota(jnp.int32, (owners, tokens), 0)
    lane = lax.broadcasted_iota(jnp.int32, (owners, LANES), 1)
    name = row_ref[...] + 1
    ids = jnp.zeros((owners, LANES), jnp.int32)
    for w in range(cap // 2):
        named = jnp.where(slot == first + 2 * w, name, 0) + jnp.where(slot == first + 2 * w + 1, name << 16, 0)
        ids = jnp.where(lane == w, jnp.sum(named, axis=1, keepdims=True), ids)
    ids_ref[...] = ids


def slots(shard, row, owners, cap):
    return pl.pallas_call(
        functools.partial(slots_kernel, cap),
        out_shape=[
            jax.ShapeDtypeStruct((owners, LANES), jnp.int32),
            jax.ShapeDtypeStruct(shard.shape, jnp.int32),
        ],
        name="slots",
    )(shard, row)


def pack_kernel(pieces, owners, slot_ref, cot_ref, out_ref, hot, wide):
    places, tokens = hot.shape
    lines = wide.shape[1]

    @pl.when(pl.program_id(0) == 0)
    def _():
        line = lax.broadcasted_iota(jnp.int32, (places, tokens), 0)
        hot[...] = jnp.where(line == slot_ref[...], 1.0, 0.0).astype(jnp.bfloat16)

    columns = pieces * LANES
    for g in range(cot_ref.shape[1] // columns):
        placed = jnp.dot(
            hot[...], cot_ref[:, g * columns : (g + 1) * columns], preferred_element_type=jnp.float32
        )
        for c in range(pieces):
            wide[g % 2, pl.ds(c, places, stride=pieces), :] = placed[:, c * LANES : (c + 1) * LANES]
        block = wide[g % 2].astype(jnp.bfloat16)
        out_ref[g * owners : (g + 1) * owners] = block.reshape(owners, lines // owners, LANES)


def pack(slot, cotangent, groups, owners, cap):
    tokens, width = cotangent.shape
    pieces = width // groups // LANES
    places = owners * cap
    lines = places * pieces
    step = groups // 2
    return pl.pallas_call(
        functools.partial(pack_kernel, pieces, owners),
        grid=(groups // step,),
        in_specs=[
            pl.BlockSpec((1, tokens), lambda g: (0, 0)),
            pl.BlockSpec((tokens, step * pieces * LANES), lambda g: (0, g)),
        ],
        out_specs=pl.BlockSpec((step * owners, cap * pieces, LANES), lambda g: (g, 0, 0)),
        out_shape=jax.ShapeDtypeStruct((groups * owners, cap * pieces, LANES), jnp.bfloat16),
        scratch_shapes=[
            pltpu.VMEM((places, tokens), jnp.bfloat16),
            pltpu.VMEM((2, lines, LANES), jnp.float32),
        ],
        cost_estimate=pl.CostEstimate(
            flops=2 * places * tokens * width,
            bytes_accessed=2 * (tokens * width + groups * lines * LANES),
            transcendentals=0,
        ),
        name="pack",
    )(slot, cotangent)


def lookup_kernel(cap, slot_ref, words_ref, table_ref, out_ref, hot_ref, lines):
    @pl.when(pl.program_id(0) == 0)
    def _():
        place = lax.broadcasted_iota(jnp.int32, hot_ref.shape, 1)
        hot_ref[...] = jnp.where(place == to_column(slot_ref[...]), 1.0, 0.0).astype(jnp.bfloat16)

    groups = words_ref.shape[0]
    devices = out_ref.shape[0]
    rows, columns = table_ref.shape
    owners = devices // groups
    pieces = columns // LANES
    here = lax.broadcasted_iota(jnp.int32, (owners, cap // 2 * owners), 0)
    there = lax.broadcasted_iota(jnp.int32, (owners, cap // 2 * owners), 1)
    row = lax.broadcasted_iota(jnp.int32, (devices, rows), 1) + 1
    for w in range(cap // 2):
        word = jnp.concatenate(
            [
                jnp.sum(jnp.where(there == here + w * owners, words_ref[g], 0), axis=1, keepdims=True)
                for g in range(groups)
            ],
            axis=0,
        )
        for half in range(2):
            name = word >> 16 if half else word & 0xFFFF
            hot = jnp.where(name == row, 1.0, 0.0).astype(jnp.bfloat16)
            found = jnp.dot(hot, table_ref[...], preferred_element_type=jnp.float32)
            for c in range(pieces):
                line = (2 * w + half) * pieces + c
                lines[pl.ds(line, devices, stride=cap * pieces), :] = found[:, c * LANES : (c + 1) * LANES]
    out_ref[...] = lines[...].astype(jnp.bfloat16).reshape(out_ref.shape)


def lookup(slot, words, table, owners, cap):
    tokens = slot.shape[1]
    groups = words.shape[0]
    rows, columns = table.shape
    pieces = columns // LANES
    step = 2
    return pl.pallas_call(
        functools.partial(lookup_kernel, cap),
        grid=(groups // step,),
        in_specs=[
            pl.BlockSpec((1, tokens), lambda g: (0, 0)),
            pl.BlockSpec((step, 1, words.shape[2]), lambda g: (g, 0, 0)),
            pl.BlockSpec((rows, columns), lambda g: (0, 0)),
        ],
        out_specs=[
            pl.BlockSpec((step * owners, cap * pieces, LANES), lambda g: (g, 0, 0)),
            pl.BlockSpec((tokens, owners * cap), lambda g: (0, 0)),
        ],
        out_shape=[
            jax.ShapeDtypeStruct((groups * owners, cap * pieces, LANES), jnp.bfloat16),
            jax.ShapeDtypeStruct((tokens, owners * cap), jnp.bfloat16),
        ],
        scratch_shapes=[pltpu.VMEM((step * owners * cap * pieces, LANES), jnp.float32)],
        cost_estimate=pl.CostEstimate(
            flops=2 * groups * owners * cap * rows * columns,
            bytes_accessed=2 * (rows * columns + groups * owners * cap * columns),
            transcendentals=0,
        ),
        name="lookup",
    )(slot, words, table)


def unpack_kernel(pieces, hot_ref, got_ref, out_ref, wide):
    places = hot_ref.shape[1]
    lines = wide.shape[1]
    columns = pieces * LANES
    groups = out_ref.shape[1] // columns
    owners = got_ref.shape[0] // groups
    for g in range(groups):
        wide[g % 2] = got_ref[g * owners : (g + 1) * owners].reshape(lines, LANES).astype(jnp.float32)
        rows = jnp.concatenate(
            [wide[g % 2, pl.ds(c, places, stride=pieces), :].astype(jnp.bfloat16) for c in range(pieces)], axis=1
        )
        picked = jnp.dot(hot_ref[...], rows, preferred_element_type=jnp.float32)
        out_ref[:, g * columns : (g + 1) * columns] = picked.astype(jnp.bfloat16)


def unpack(hot, got, groups, width):
    tokens = hot.shape[0]
    pieces = width // groups // LANES
    owners = got.shape[0] // groups
    lines = owners * got.shape[1]
    step = groups // 2
    return pl.pallas_call(
        functools.partial(unpack_kernel, pieces),
        grid=(groups // step,),
        in_specs=[
            pl.BlockSpec(hot.shape, lambda g: (0, 0)),
            pl.BlockSpec((step * owners, got.shape[1], LANES), lambda g: (g, 0, 0)),
        ],
        out_specs=pl.BlockSpec((tokens, step * pieces * LANES), lambda g: (0, g)),
        out_shape=jax.ShapeDtypeStruct((tokens, width), jnp.bfloat16),
        scratch_shapes=[pltpu.VMEM((2, lines, LANES), jnp.float32)],
        name="unpack",
    )(hot, got)


def exchange(x, axes):
    return lax.all_to_all(x, axes, split_axis=0, concat_axis=0, tiled=True)


def per_device(shard_ids, row_ids, table, cotangent):
    tokens, width = cotangent.shape
    groups = lax.axis_size("group")
    owners = lax.axis_size("vocab")
    cap = 2 * tokens // owners
    peers = groups * owners
    rows_here, columns = table.shape
    outgoing, slot = slots(shard_ids.reshape(1, tokens), row_ids.reshape(1, tokens), owners, cap)
    ids = exchange(outgoing.reshape(owners, 1, LANES), "vocab")
    packed = pack(slot, cotangent, groups, owners, cap)
    ids, packed = lax.optimization_barrier((ids, packed))
    arrived = exchange(packed, ("group", "vocab"))
    mine = jnp.swapaxes(ids[:, 0, : cap // 2], 0, 1).reshape(1, cap // 2 * owners)
    words = lax.all_gather(mine, "group", axis=0)
    found, hot = lookup(slot, words, table, owners, cap)
    got = exchange(found, ("group", "vocab"))
    words = words.reshape(groups, cap // 2, owners)
    wanted = jnp.stack([words & 0xFFFF, words >> 16], axis=2).reshape(groups, cap, owners)
    wanted = jnp.swapaxes(wanted, 1, 2).reshape(-1) - 1
    picker = (wanted[:, None] == jnp.arange(rows_here, dtype=jnp.int32)[None, :]).astype(jnp.bfloat16)
    table_grad = lax.dot_general(
        picker,
        arrived.reshape(peers * cap, columns),
        (((0,), (0,)), ((), ())),
        preferred_element_type=jnp.float32,
    )
    embeds = unpack(hot, got, groups, width)
    return (embeds, table_grad.astype(jnp.bfloat16))


def solution(mesh):
    in_specs = (
        P(("group", "vocab"), None),
        P(("group", "vocab")),
        P("vocab", "group"),
        P(("group", "vocab"), None),
    )
    out_specs = (P(("group", "vocab"), None), P("vocab", "group"))
    return jax.shard_map(
        per_device, mesh=mesh, in_specs=in_specs, out_specs=out_specs, check_vma=False
    )
```
